256 devices in a mesh: dp: 16 (over z_lo, y, core), mp: 16 (over x, z_hi).
Axes of the slice: x: 4, y: 4, z: 8 (z_hi: 4, z_lo: 2; z = z_hi * 2 + z_lo), core: 2. Of those that a mesh axis runs over, the one named last changes fastest.
Arguments:
- tokens: bfloat16 [2048, 4096], P('dp', 'mp'), may hold values from -6 to 6
- cotangent: bfloat16 [2048, 4096], P('dp', 'mp'), may hold values from -6 to 6
- block_cols: int32 [64, 32], replicated, may hold values from 0 to 255, as said below
- in_weights: bfloat16 [4096, 4096], P('mp'), may hold values from -0.25 to 0.25
- out_weights: bfloat16 [4096, 4096], P('mp'), may hold values from -0.125 to 0.125
Outputs:
- layer_out: bfloat16 [2048, 4096], P('dp', 'mp')
- token_grad: bfloat16 [2048, 4096], P('dp', 'mp')
- in_weight_grad: float32 [4096, 4096], P(('mp', 'dp'))
- out_weight_grad: float32 [4096, 4096], P(('mp', 'dp'))
The draws below stay inside these ranges and needn't reach their ends.
Inputs may be any that keep to these rules, and one draw needn't show every extreme that they name: `block_cols`: each row lists 32 different hidden blocks in increasing order. The entries naming hidden blocks of one hidden group number at most 256, and exactly 256 for one group in every draw; one row has at most 4 entries in one hidden group.
All inputs are finite; a program needn't handle non-finite values.
Results may differ from the reference program's by a relative error of at most 0.017.
Values may be sent and summed in bfloat16 or wider, within the bound.
No kernel may reach another device: no remote copies, remote signals or barrier semaphores. Data moves between devices by JAX's collectives and lax.ppermute only.
A program may use at most 128 MiB of HBM per device.

```python
import math
import jax
import jax.numpy as jnp
from jax import lax

D = 4096
FF = 16384
BLK = 64
TOK = 128
TOKENS = 2048
DB = 64
HBL = 16
CAP = 256
SLOTS = 4096
N_DP = 16
N_MP = 16


def draw_block_cols(key, part):
    key_hot, key_rank, key_pick = jax.random.split(key, 3)
    hidden_blocks = FF // BLK
    local_blocks = HBL
    model_parts = hidden_blocks // local_blocks
    per_row = hidden_blocks // 8
    base_share = per_row // model_parts
    row_count = D // BLK
    hot_part = jax.random.randint(key_hot, (), 0, model_parts)
    within_ids = jnp.arange(local_blocks, dtype=jnp.int32)
    rank_keys = jax.random.randint(key_rank, (row_count, model_parts, local_blocks), 0, 1 << 20) * local_blocks + within_ids
    within = jnp.argsort(jnp.argsort(rank_keys, axis=2), axis=2)
    candidate = within < 2 * base_share
    is_hot = (jnp.arange(model_parts, dtype=jnp.int32) == hot_part)[None, :, None]
    serial = jnp.arange(hidden_blocks, dtype=jnp.int32).reshape(1, model_parts, local_blocks)
    pick_keys = jax.random.randint(key_pick, (row_count, model_parts, local_blocks), 0, 1 << 20) * hidden_blocks + serial
    pick_keys = jnp.where(candidate & ~is_hot, pick_keys, (1 << 30) + serial)
    flat_keys = pick_keys.reshape(row_count, hidden_blocks)
    picked = jnp.argsort(jnp.argsort(flat_keys, axis=1), axis=1) < (model_parts - 2) * base_share
    chosen = (candidate & is_hot).reshape(row_count, hidden_blocks) | picked
    block_ids = jnp.arange(hidden_blocks, dtype=jnp.int32)[None, :]
    order_keys = jnp.where(chosen, block_ids, hidden_blocks + block_ids)
    return jnp.sort(order_keys, axis=1)[:, :per_row].astype(jnp.int32)


def shard_levels(own_key, shape, cuts, low, top_value):
    loudness = 1.0
    for axis_at, shards_of in cuts:
        heights = jax.random.uniform(jax.random.fold_in(jax.random.fold_in(own_key, 6), axis_at), (shards_of,), jnp.float32, low / len(cuts), top_value / len(cuts))
        loudness = loudness * jnp.repeat(jnp.exp(heights), shape[axis_at] // shards_of).reshape((-1,) + (1,) * (len(shape) - 1 - axis_at))
    return loudness


def centred(own_key, extent, deviation, limit, pieces=(), kind=jnp.bfloat16):
    array = jax.random.normal(own_key, extent, jnp.float32) * deviation
    if len(pieces) > 0:
        array = shard_levels(own_key, extent, pieces, -0.22, 0.18) * array
    return jnp.clip(array, min=-limit, max=limit).astype(kind)


def setup_inputs(seed: int = 0) -> dict:
    key_of = jax.random.split(jax.random.key(seed), 6)
    tokens = centred(key_of[0], (TOKENS, D), 1.0, 6.0, ((0, 16), (1, 16)))
    cotangent = centred(key_of[1], (TOKENS, D), 1.0, 6.0, ((0, 16), (1, 16)))
    block_cols = draw_block_cols(jax.random.fold_in(key_of[5], 71), 0)
    in_weights = centred(key_of[3], (SLOTS, BLK * BLK), (D // 8) ** -0.5, 0.25, ((0, 16),))
    out_weights = centred(key_of[4], (SLOTS, BLK * BLK), (FF // 8) ** -0.5, 0.125, ((0, 16),))
    return {"tokens": tokens, "cotangent": cotangent, "block_cols": block_cols, "in_weights": in_weights, "out_weights": out_weights}


def slot_tables(block_cols, my_shard, slot_count, local_blocks):
    row_count = block_cols.shape[0]
    per_row = block_cols.shape[1]
    flat_cols = block_cols.reshape(-1).astype(jnp.int32)
    is_mine = flat_cols // local_blocks == my_shard
    ranks = jnp.cumsum(is_mine.astype(jnp.int32), dtype=jnp.int32) - 1
    targets = jnp.where(is_mine, ranks, slot_count).astype(jnp.int32)
    row_ids = (jnp.arange(flat_cols.shape[0], dtype=jnp.int32) // per_row).astype(jnp.int32)
    slot_row = jnp.full((slot_count,), row_count, jnp.int32).at[targets].set(row_ids, mode='drop')
    local_cols = (flat_cols - my_shard * local_blocks).astype(jnp.int32)
    slot_col = jnp.full((slot_count,), local_blocks, jnp.int32).at[targets].set(local_cols, mode='drop')
    return (slot_row, slot_col)

def gather_blocks(matrix, indices):
    row_total = matrix.shape[0]
    return jnp.take(matrix.reshape(row_total, -1, BLK), indices, axis=1, mode='fill', fill_value=0)

def sum_blocks(block_terms, indices, block_count):
    summed = jax.ops.segment_sum(block_terms, indices, num_segments=block_count)
    return jnp.transpose(summed, (1, 0, 2)).reshape(block_terms.shape[1], block_count * BLK)

def gelu_tanh(values):
    return jax.nn.gelu(values, approximate=True)

def shard_terms(feature_rows, grad_rows, slot_row, slot_col, in_blocks, out_blocks):
    in_wide = in_blocks.astype(jnp.float32)
    out_wide = out_blocks.astype(jnp.float32)
    token_blocks = gather_blocks(feature_rows, slot_row)
    pre_terms = jnp.einsum('tsi,sij->stj', token_blocks.astype(jnp.float32), in_wide)
    hidden = sum_blocks(pre_terms, slot_col, HBL)
    activated = gelu_tanh(hidden).astype(jnp.bfloat16)
    act_blocks = gather_blocks(activated, slot_col)
    out_part = sum_blocks(jnp.einsum('tsi,sij->stj', act_blocks.astype(jnp.float32), out_wide), slot_row, DB)
    grad_blocks = gather_blocks(grad_rows, slot_row)
    act_grad = sum_blocks(jnp.einsum('tsj,sij->sti', grad_blocks.astype(jnp.float32), out_wide), slot_col, HBL)
    pullback = jax.vjp(gelu_tanh, hidden)[1]
    pre_grad = pullback(act_grad)[0].astype(jnp.bfloat16)
    pre_blocks = gather_blocks(pre_grad, slot_col)
    in_part = sum_blocks(jnp.einsum('tsj,sij->sti', pre_blocks.astype(jnp.float32), in_wide), slot_row, DB)
    out_term = jnp.einsum('tsi,tsj->sij', act_blocks.astype(jnp.float32), grad_blocks.astype(jnp.float32))
    in_term = jnp.einsum('tsi,tsj->sij', token_blocks.astype(jnp.float32), pre_blocks.astype(jnp.float32))
    return (out_part, in_part, in_term, out_term)

def reference(tokens, cotangent, block_cols, in_weights, out_weights):
    shard_ids = jnp.arange(N_MP, dtype=jnp.int32)

    def tables_of(shard_index):
        return slot_tables(block_cols, shard_index, CAP, HBL)
    rows_all, cols_all = jax.vmap(tables_of)(shard_ids)
    in_all = in_weights.reshape(N_MP, CAP, BLK, BLK)
    out_all = out_weights.reshape(N_MP, CAP, BLK, BLK)
    grad_scale = 1.0 / math.sqrt(TOKENS)
    token_groups = tokens.reshape(N_DP, TOK, D)
    grad_groups = cotangent.reshape(N_DP, TOK, D)

    def one_group(totals, group_pair):
        in_total, out_total = totals
        feature_rows, grad_rows = group_pair

        def one_shard(shard_items):
            return shard_terms(feature_rows, grad_rows, shard_items[0], shard_items[1], shard_items[2], shard_items[3])
        out_parts, in_parts, in_terms, out_terms = lax.map(one_shard, (rows_all, cols_all, in_all, out_all))
        layer_out = lax.optimization_barrier(jnp.sum(lax.optimization_barrier(out_parts.astype(jnp.bfloat16)).astype(jnp.float32), axis=0)).astype(jnp.bfloat16)
        token_grad = lax.optimization_barrier(jnp.sum(lax.optimization_barrier(in_parts.astype(jnp.bfloat16)).astype(jnp.float32), axis=0)).astype(jnp.bfloat16)
        in_total = in_total + lax.optimization_barrier((grad_scale * in_terms).astype(jnp.bfloat16)).astype(jnp.float32)
        out_total = out_total + lax.optimization_barrier((grad_scale * out_terms).astype(jnp.bfloat16)).astype(jnp.float32)
        return ((in_total, out_total), (layer_out, token_grad))
    empty_grads = jnp.zeros((N_MP, CAP, BLK, BLK), jnp.float32)
    final, outputs = lax.scan(one_group, (empty_grads, empty_grads), (token_groups, grad_groups))
    return (outputs[0].reshape(TOKENS, D), outputs[1].reshape(TOKENS, D), final[0].reshape(SLOTS, BLK * BLK), final[1].reshape(SLOTS, BLK * BLK))
```

```python
import functools

import jax
import jax.numpy as jnp
from jax import lax
from jax.experimental import pallas as pl
from jax.experimental.pallas import tpu as pltpu
from jax.sharding import PartitionSpec as P

D = 4096
FF = 16384
BLK = 64
HBL = 16
VMEM_LIMIT = 60 * 1024 * 1024


def place_of(steps):
    d = steps % 4
    return jnp.where(d == 0, 0, jnp.where(d == 3, 1, jnp.where(d == 1, 2, 3)))


def steps_of(place):
    return jnp.where(place == 0, 0, jnp.where(place == 1, 3, jnp.where(place == 2, 1, 2)))


def slot_tables(block_cols, mp_at, dp_at, slot_count):
    row_count, per_row = block_cols.shape
    flat_cols = block_cols.reshape(1, -1)
    is_mine = flat_cols // HBL == mp_at
    ranks = jnp.cumsum(is_mine.astype(jnp.int32), axis=1, dtype=jnp.int32) - 1
    targets = jnp.where(is_mine, ranks, slot_count)
    row_ids = lax.broadcasted_iota(jnp.int32, flat_cols.shape, 1) // per_row
    packed = row_ids * HBL + flat_cols - mp_at * HBL + 1
    slots = lax.broadcasted_iota(jnp.int32, (slot_count, 1), 0)
    found = jnp.sum(jnp.where(targets == slots, packed, 0), axis=1, dtype=jnp.int32)
    entry = jnp.where(found > 0, found - 1, row_count * HBL)
    run = lax.broadcasted_iota(jnp.int32, (16, 1), 0)
    owner = (mp_at // 4 + steps_of(run // 4)) % 4 * 4 + (mp_at % 4 + steps_of(run % 4)) % 4
    first = jnp.sum((entry[None, :] < owner * (4 * HBL)).astype(jnp.int32), axis=1, dtype=jnp.int32)
    last = jnp.sum((entry[None, :] < (owner + 1) * (4 * HBL)).astype(jnp.int32), axis=1, dtype=jnp.int32)
    row = entry // HBL
    at = place_of(row // 16 - mp_at // 4) * 4 + place_of(row // 4 - mp_at % 4)
    dest = jnp.where(entry < row_count * HBL, (at * 4 + row % 4) * HBL + entry % HBL, row_count * HBL)
    slot = slots[:, 0]
    to = slot // 16
    core, across, deep = (to + dp_at) % 2, place_of(to // 2 - dp_at // 2 % 4), (to // 8 + dp_at // 8) % 2
    send = ((core * 4 + across) * 2 + deep) * 16 + slot % 16
    return dest, send, first, last


def dense_kernel(turned, dest, w_ref, d_ref, lines):
    d_ref[...] = jnp.zeros_like(d_ref)
    at_once = 16
    count = at_once // 2 if turned else at_once
    low = lax.broadcasted_iota(jnp.int32, (count, 2 * BLK), 1) < BLK
    upper = lax.broadcasted_iota(jnp.int32, (BLK, 2 * BLK), 1) >= BLK

    def place(e, block):
        c = e % HBL
        here = d_ref.at[c // 2, pl.ds(pl.multiple_of(e // HBL * BLK, BLK), BLK), :]
        here[...] = jnp.where(upper == (c % 2 == 1), block.astype(jnp.bfloat16), here[...])

    def some(k, carry):
        start = pl.multiple_of(k * at_once, at_once)
        for t in range(BLK // 2):
            two = w_ref[pl.ds(start, at_once), 2 * BLK * t : 2 * BLK * (t + 1)].astype(jnp.float32)
            swapped = pltpu.roll(two, BLK, 1)
            if turned:
                even = jnp.where(low, two[:count], swapped[count:])
                odd = jnp.where(low, swapped[:count], two[count:])
            else:
                even, odd = jnp.where(low, two, swapped), jnp.where(low, swapped, two)
            lines[pl.ds(2 * t, count, stride=BLK), :] = even
            lines[pl.ds(2 * t + 1, count, stride=BLK), :] = odd
        for u in range(count):
            block = lines[u * BLK : (u + 1) * BLK, :]
            if turned:
                both = jnp.concatenate([block, block], axis=0).T
                place(dest[start + u], both[:BLK])
                place(dest[start + u + count], both[BLK:])
            else:
                place(dest[start + u], block)
        return carry

    lax.fori_loop(0, dest.shape[0] // at_once, some, 0)


def dense_weights(dest, weights, turned):
    whole = pl.BlockSpec(memory_space=pltpu.VMEM)
    return pl.pallas_call(
        functools.partial(dense_kernel, turned),
        out_shape=jax.ShapeDtypeStruct((8, D + BLK, 2 * BLK), jnp.bfloat16),
        in_specs=[pl.BlockSpec(memory_space=pltpu.SMEM), whole],
        out_specs=whole,
        scratch_shapes=[pltpu.VMEM((16 * BLK, 2 * BLK), jnp.float32)],
        compiler_params=pltpu.CompilerParams(vmem_limit_bytes=VMEM_LIMIT),
        cost_estimate=pl.CostEstimate(flops=0, transcendentals=0, bytes_accessed=20 << 20),
        name="dense_out" if turned else "dense_in",
    )(dest, weights)


def hidden_kernel(xc_ref, din_ref, dout_ref, act_ref, pre_ref):
    tok = xc_ref.shape[1] // 2
    x = jnp.concatenate([xc_ref[j, :tok, :] for j in range(16)], axis=1)
    c = jnp.concatenate([xc_ref[j, tok:, :] for j in range(16)], axis=1)
    win = jnp.concatenate([din_ref[0], din_ref[1]], axis=1)
    wout = jnp.concatenate([dout_ref[0], dout_ref[1]], axis=1)
    v = jnp.dot(x, win, preferred_element_type=jnp.float32)
    g = jnp.dot(c, wout, preferred_element_type=jnp.float32)
    k0 = 0.7978845608028654
    t = jnp.tanh(k0 * (v + 0.044715 * (v * v * v)))
    act_ref[...] = (0.5 * v * (1.0 + t)).T.astype(jnp.bfloat16)
    slope = 0.5 * (1.0 + t) + 0.5 * v * (1.0 - t * t) * (k0 * (1.0 + 3 * 0.044715 * (v * v)))
    pre_ref[...] = (g * slope).T.astype(jnp.bfloat16)


def hidden_stage(xc, din, dout, tok):
    cost = pl.CostEstimate(flops=4 * tok * D * 1024, transcendentals=tok * 1024, bytes_accessed=18 << 20)
    wide = pl.BlockSpec((2, D, 2 * BLK), lambda q: (q, 0, 0))
    tall = pl.BlockSpec((4 * BLK, tok), lambda q: (q, 0))
    shape = jax.ShapeDtypeStruct((1024, tok), jnp.bfloat16)
    return pl.pallas_call(
        hidden_kernel,
        grid=(4,),
        out_shape=(shape, shape),
        in_specs=[pl.BlockSpec(xc.shape, lambda q: (0, 0, 0)), wide, wide],
        out_specs=(tall, tall),
        compiler_params=pltpu.CompilerParams(vmem_limit_bytes=VMEM_LIMIT),
        cost_estimate=cost,
        name="hidden_stage",
    )(xc, din, dout)


def grad_kernel(scale, dest, send, first, last, xc_ref, act_ref, pre_ref, own_ref, other_ref, g_scr, in_scr, out_scr):
    j = pl.program_id(0)
    tok = act_ref.shape[1]
    at_once = 4

    @pl.when(j == 0)
    def _():
        g_scr[...] = jnp.zeros_like(g_scr)

    gin = jnp.dot(pre_ref[...], xc_ref[0, :tok, :], preferred_element_type=jnp.float32)
    gout = jnp.dot(act_ref[...], xc_ref[0, tok:, :], preferred_element_type=jnp.float32)
    for half in range(2):
        in_scr[half] = gin[:, half * 128 : half * 128 + 128]
        out_scr[half] = gout[:, half * 128 : half * 128 + 128]
    upper = lax.broadcasted_iota(jnp.int32, (BLK, 2 * BLK), 1) >= BLK
    begin, end = first[j], last[j]

    def take(i, carry):
        found = []
        for u in range(at_once):
            s = jnp.minimum(begin + i * at_once + u, end - 1)
            e = dest[s]
            r, c = e // HBL % 4, e % HBL
            tile, odd = r // 2, r % 2
            rows = pl.ds(pl.multiple_of(c * BLK, BLK), BLK)
            low = pltpu.roll(out_scr[tile, rows, :], odd * BLK, 1)
            high = pltpu.roll(in_scr[tile, rows, :], (1 - odd) * BLK, 1)
            found.append((send[s], (jnp.where(upper, high, low) * scale).astype(jnp.bfloat16)))
        for to, block in found:
            g_scr[to] = block
        return carry

    lax.fori_loop(0, (end - begin + at_once - 1) // at_once, take, 0)

    @pl.when(j == pl.num_programs(0) - 1)
    def _():
        half = own_ref.shape[0]
        own_ref[...] = g_scr[:half]
        other_ref[...] = g_scr[half:]


def grad_stage(tables, xc, act, pre, slot_count, scale):
    tok = act.shape[1]
    cost = pl.CostEstimate(flops=4 * tok * D * 1024, transcendentals=0, bytes_accessed=7 << 20)
    whole = pl.BlockSpec(act.shape, lambda j: (0, 0))
    smem = pl.BlockSpec(memory_space=pltpu.SMEM)
    half = (slot_count // 2, BLK, 2 * BLK)
    half_spec = pl.BlockSpec(half, lambda j: (0, 0, 0), pipeline_mode=pl.Buffered(1))
    return pl.pallas_call(
        functools.partial(grad_kernel, scale),
        grid=(16,),
        out_shape=(jax.ShapeDtypeStruct(half, jnp.bfloat16),) * 2,
        in_specs=[smem] * 4 + [pl.BlockSpec((1,) + xc.shape[1:], lambda j: (j, 0, 0)), whole, whole],
        out_specs=(half_spec, half_spec),
        scratch_shapes=[pltpu.VMEM((slot_count, BLK, 2 * BLK), jnp.bfloat16)]
        + [pltpu.VMEM((2, 1024, 128), jnp.float32)] * 2,
        compiler_params=pltpu.CompilerParams(vmem_limit_bytes=VMEM_LIMIT),
        cost_estimate=cost,
        name="grad_stage",
    )(*tables, xc, act, pre)


def part_kernel(din_ref, dout_ref, act_ref, pre_ref, *part_refs):
    j = pl.program_id(0)
    win = jnp.concatenate([din_ref[p] for p in range(8)], axis=1)
    wout = jnp.concatenate([dout_ref[p] for p in range(8)], axis=1)
    out = jnp.dot(wout, act_ref[...], preferred_element_type=jnp.float32).astype(jnp.bfloat16)
    back = jnp.dot(win, pre_ref[...], preferred_element_type=jnp.float32).astype(jnp.bfloat16)
    both = jnp.concatenate([out, back], axis=1)
    for n, ref in enumerate(part_refs):

        @pl.when(j // 2 == n)
        def _():
            ref[...] = both


def part_stage(din, dout, act, pre):
    tok = act.shape[1]
    cost = pl.CostEstimate(flops=4 * tok * D * 1024, transcendentals=0, bytes_accessed=18 << 20)
    whole = pl.BlockSpec(act.shape, lambda j: (0, 0))
    wide = pl.BlockSpec((8, 512, 2 * BLK), lambda j: (0, j, 0))
    pieces = tuple(
        pl.BlockSpec((512, 2 * tok), lambda j, n=n: (jnp.clip(j - 2 * n, 0, 1), 0)) for n in range(4)
    )
    return pl.pallas_call(
        part_kernel,
        grid=(D // 512,),
        out_shape=(jax.ShapeDtypeStruct((1024, 2 * tok), jnp.bfloat16),) * 4,
        in_specs=[wide, wide, whole, whole],
        out_specs=pieces,
        compiler_params=pltpu.CompilerParams(vmem_limit_bytes=VMEM_LIMIT),
        cost_estimate=cost,
        name="part_stage",
    )(din, dout, act, pre)


def total_kernel(own_ref, before_ref, after_ref, opposite_ref, out_ref, back_ref):
    refs = (own_ref, before_ref, after_ref, opposite_ref)
    total = sum(ref[...].astype(jnp.float32) for ref in refs)
    tok = out_ref.shape[0]
    out_ref[...] = total[:, :tok].T.astype(jnp.bfloat16)
    back_ref[...] = total[:, tok:].T.astype(jnp.bfloat16)


def total_turned(terms):
    rows, cols = terms[0].shape
    return pl.pallas_call(
        total_kernel,
        out_shape=(jax.ShapeDtypeStruct((cols // 2, rows), jnp.bfloat16),) * 2,
        name="total_turned",
    )(*terms)


def ring(axis, stride):
    def target(i, by):
        return i - i // stride % 4 * stride + (i // stride + by) % 4 * stride

    return tuple(
        functools.partial(lax.ppermute, axis_name=axis, perm=[(i, target(i, by)) for i in range(16)])
        for by in (1, 3, 2)
    )


def spread(block, up, down, over):
    return jnp.stack([block, up(block), down(block), over(block)])


def collect(blocks, up, down, over):
    own, before, after, opposite = blocks
    return own, up(after), down(before), over(opposite)


def added(*terms):
    return sum(term.astype(jnp.float32) for term in terms).astype(jnp.bfloat16)


def on_device(tokens, cotangent, block_cols, in_weights, out_weights):
    mp_at, dp_at = lax.axis_index("mp"), lax.axis_index("dp")
    slot_count = in_weights.shape[0]
    tok = tokens.shape[0]
    scale = float(tok * lax.axis_size("dp")) ** (-0.5)
    along_x, along_z, along_y = ring("mp", 4), ring("mp", 1), ring("dp", 2)
    block = jnp.concatenate([tokens, cotangent], axis=0)
    near = spread(block, *along_z)
    tables = slot_tables(block_cols, mp_at, dp_at, slot_count)
    din = dense_weights(tables[0], in_weights, False)
    near, din = lax.optimization_barrier((near, din))
    xc = spread(near, *along_x).reshape(16, 2 * tok, -1)
    dout = dense_weights(tables[0], out_weights, True)
    act, pre = hidden_stage(xc, din, dout, tok)
    mine, other = grad_stage(tables, xc, act, pre, slot_count, scale)
    from_core = lax.ppermute(other, "dp", [(i, i ^ 1) for i in range(16)])
    parts = part_stage(din, dout, act, pre)
    parts, from_core = lax.optimization_barrier((parts, from_core))
    share = slot_count // 8
    pair = [
        added(mine[n * share : (n + 1) * share], from_core[n * share : (n + 1) * share]) for n in range(4)
    ]
    deep_terms = collect(pair, *along_y)
    across_terms = collect(parts, *along_x)
    deep_terms, across_terms = lax.optimization_barrier((deep_terms, across_terms))
    half = share // 2
    from_deep = lax.ppermute(added(*(term[half:] for term in deep_terms)), "dp", [(i, i ^ 8) for i in range(16)])
    rows = across_terms[0].shape[0] // 4
    across = [added(*(term[n * rows : (n + 1) * rows] for term in across_terms)) for n in range(4)]
    layer_out, token_grad = total_turned(collect(across, *along_z))
    summed = sum(term[:half].astype(jnp.float32) for term in deep_terms) + from_deep.astype(jnp.float32)
    out_grad = summed[:, :, :BLK].reshape(-1, BLK * BLK)
    in_grad = summed[:, :, BLK:].swapaxes(1, 2).reshape(-1, BLK * BLK)
    return (layer_out, token_grad, in_grad, out_grad)


def solution(mesh):
    placed = (P("dp", "mp"), P("dp", "mp"), P(), P("mp", None), P("mp", None))
    return jax.shard_map(
        on_device,
        mesh=mesh,
        in_specs=placed,
        out_specs=(P("dp", "mp"), P("dp", "mp"), P(("mp", "dp"), None), P(("mp", "dp"), None)),
        check_vma=False,
    )
```

```python
import functools

import jax
import jax.numpy as jnp
from jax import lax
from jax.experimental import pallas as pl
from jax.experimental.pallas import tpu as pltpu
from jax.sharding import PartitionSpec as P


D = 4096
BLK = 64
HBL = 16
MIB = 1024 * 1024


def place_of(steps):
    d = steps % 4
    return jnp.where(d == 0, 0, jnp.where(d == 3, 1, jnp.where(d == 1, 2, 3)))


def steps_of(place):
    return jnp.where(place == 0, 0, jnp.where(place == 1, 3, jnp.where(place == 2, 1, 2)))


def slot_tables(block_cols, mp_at, dp_at, slot_count):
    row_count, per_row = block_cols.shape
    flat_cols = block_cols.reshape(1, -1)
    is_mine = flat_cols // HBL == mp_at
    ranks = jnp.cumsum(is_mine.astype(jnp.int32), axis=1, dtype=jnp.int32) - 1
    targets = jnp.where(is_mine, ranks, slot_count)
    row_ids = lax.broadcasted_iota(jnp.int32, flat_cols.shape, 1) // per_row
    packed = row_ids * HBL + flat_cols - mp_at * HBL + 1
    slots = lax.broadcasted_iota(jnp.int32, (slot_count, 1), 0)
    found = jnp.sum(jnp.where(targets == slots, packed, 0), axis=1, dtype=jnp.int32)
    entry = jnp.where(found > 0, found - 1, row_count * HBL)
    place = lax.broadcasted_iota(jnp.int32, (row_count, 1), 0)
    owner = (mp_at // 4 + steps_of(place // 16)) % 4 * 4 + (mp_at % 4 + steps_of(place // 4 % 4)) % 4
    begin = (owner * 4 + place % 4) * HBL
    first = jnp.sum((entry[None, :] < begin).astype(jnp.int32), axis=1, dtype=jnp.int32)
    last = jnp.sum((entry[None, :] < begin + HBL).astype(jnp.int32), axis=1, dtype=jnp.int32)
    row = entry // HBL
    at = place_of(row // 16 - mp_at // 4) * 4 + place_of(row // 4 - mp_at % 4)
    dest = jnp.where(entry < row_count * HBL, (at * 4 + row % 4) * HBL + entry % HBL, row_count * HBL)
    slot = slots[:, 0]
    to = slot // 16
    core, across, deep = (to + dp_at) % 2, place_of(to // 2 - dp_at // 2 % 4), (to // 8 + dp_at // 8) % 2
    send = ((core * 4 + across) * 2 + deep) * 16 + slot % 16
    return dest, send, first, last


def dense_kernel(turned, dest, w_ref, d_ref, lines):
    d_ref[...] = jnp.zeros_like(d_ref)
    at_once = 16
    count = at_once // 2 if turned else at_once
    low = lax.broadcasted_iota(jnp.int32, (count, 2 * BLK), 1) < BLK
    upper = lax.broadcasted_iota(jnp.int32, (BLK, 2 * BLK), 1) >= BLK

    def place(e, block):
        c = e % HBL
        here = d_ref.at[c // 2, pl.ds(pl.multiple_of(e // HBL * BLK, BLK), BLK), :]
        here[...] = jnp.where(upper == (c % 2 == 1), block.astype(jnp.bfloat16), here[...])

    def some(k, carry):
        start = pl.multiple_of(k * at_once, at_once)
        for t in range(BLK // 2):
            two = w_ref[pl.ds(start, at_once), 2 * BLK * t : 2 * BLK * (t + 1)].astype(jnp.float32)
            swapped = pltpu.roll(two, BLK, 1)
            if turned:
                even = jnp.where(low, two[:count], swapped[count:])
                odd = jnp.where(low, swapped[:count], two[count:])
            else:
                even, odd = jnp.where(low, two, swapped), jnp.where(low, swapped, two)
            lines[pl.ds(2 * t, count, stride=BLK), :] = even
            lines[pl.ds(2 * t + 1, count, stride=BLK), :] = odd
        for u in range(count):
            block = lines[u * BLK : (u + 1) * BLK, :]
            if turned:
                both = jnp.concatenate([block, block], axis=0).T
                place(dest[start + u], both[:BLK])
                place(dest[start + u + count], both[BLK:])
            else:
                place(dest[start + u], block)
        return carry

    lax.fori_loop(0, dest.shape[0] // at_once, some, 0)


def dense_weights(dest, weights, turned):
    whole = pl.BlockSpec(memory_space=pltpu.VMEM)
    return pl.pallas_call(
        functools.partial(dense_kernel, turned),
        out_shape=jax.ShapeDtypeStruct((8, D + BLK, 2 * BLK), jnp.bfloat16),
        in_specs=[pl.BlockSpec(memory_space=pltpu.SMEM), whole],
        out_specs=whole,
        scratch_shapes=[pltpu.VMEM((16 * BLK, 2 * BLK), jnp.float32)],
        compiler_params=pltpu.CompilerParams(vmem_limit_bytes=14 * MIB),
        cost_estimate=pl.CostEstimate(flops=0, transcendentals=0, bytes_accessed=20 << 20),
        name="dense_out" if turned else "dense_in",
    )(dest, weights)


def hidden_kernel(xc_ref, din_ref, dout_ref, both_ref):
    tok = xc_ref.shape[1] // 2
    x = jnp.concatenate([xc_ref[j, :tok, :] for j in range(16)], axis=1)
    c = jnp.concatenate([xc_ref[j, tok:, :] for j in range(16)], axis=1)
    win = jnp.concatenate([din_ref[0], din_ref[1]], axis=1)
    wout = jnp.concatenate([dout_ref[0], dout_ref[1]], axis=1)
    v = jnp.dot(x, win, preferred_element_type=jnp.float32)
    g = jnp.dot(c, wout, preferred_element_type=jnp.float32)
    k0 = 0.7978845608028654
    t = jnp.tanh(k0 * (v + 0.044715 * (v * v * v)))
    both_ref[:, tok:] = (0.5 * v * (1.0 + t)).T.astype(jnp.bfloat16)
    slope = 0.5 * (1.0 + t) + 0.5 * v * (1.0 - t * t) * (k0 * (1.0 + 3 * 0.044715 * (v * v)))
    both_ref[:, :tok] = (g * slope).T.astype(jnp.bfloat16)


def hidden_stage(xc, din, dout, tok):
    cost = pl.CostEstimate(flops=4 * tok * D * 1024, transcendentals=tok * 1024, bytes_accessed=18 << 20)
    wide = pl.BlockSpec((2, D, 2 * BLK), lambda q: (q, 0, 0))
    return pl.pallas_call(
        hidden_kernel,
        grid=(4,),
        out_shape=jax.ShapeDtypeStruct((1024, 2 * tok), jnp.bfloat16),
        in_specs=[pl.BlockSpec(xc.shape, lambda q: (0, 0, 0)), wide, wide],
        out_specs=pl.BlockSpec((4 * BLK, 2 * tok), lambda q: (q, 0)),
        compiler_params=pltpu.CompilerParams(vmem_limit_bytes=26 * MIB),
        cost_estimate=cost,
        name="hidden_stage",
    )(xc, din, dout)


def grad_kernel(scale, dest, send, first, last, xc_ref, both_ref, own_ref, other_ref, g_scr):
    j = pl.program_id(0)
    tok = both_ref.shape[1] // 2
    unused = g_scr.shape[0] - 1
    most = 4

    @pl.when(j == 0)
    def _():
        g_scr[...] = jnp.zeros_like(g_scr)

    upper = lax.broadcasted_iota(jnp.int32, (tok, 2 * BLK), 1) >= BLK
    for q in range(4):
        begin, end = first[j * 4 + q], last[j * 4 + q]
        tile = xc_ref[0, :, q // 2 * 2 * BLK : (q // 2 + 1) * 2 * BLK].astype(jnp.float32)
        x, c = tile[:tok], tile[tok:]
        if q % 2:
            c = pltpu.roll(c, BLK, 1)
        else:
            x = pltpu.roll(x, BLK, 1)
        sides = jnp.concatenate([jnp.where(upper, x, 0.0), jnp.where(upper, 0.0, c)], axis=0).astype(jnp.bfloat16)
        blocks, targets = [], []
        for u in range(most):
            s = jnp.minimum(begin + u, unused - 1)
            at = pl.multiple_of(dest[s] % HBL * BLK, BLK)
            blocks.append(both_ref[pl.ds(at, BLK), :])
            targets.append(jnp.where(begin + u < end, send[s], unused))
        terms = jnp.dot(jnp.concatenate(blocks, axis=0), sides, preferred_element_type=jnp.float32)
        terms = (terms * scale).astype(jnp.bfloat16)
        for u in range(most):
            g_scr[targets[u]] = terms[u * BLK : (u + 1) * BLK]

    @pl.when(j == pl.num_programs(0) - 1)
    def _():
        half = own_ref.shape[0]
        own_ref[...] = g_scr[:half]
        other_ref[...] = g_scr[half : 2 * half]


def grad_stage(tables, xc, both, slot_count, scale):
    tok = both.shape[1] // 2
    cost = pl.CostEstimate(flops=tok * D * 1024, transcendentals=0, bytes_accessed=7 << 20)
    smem = pl.BlockSpec(memory_space=pltpu.SMEM)
    half = (slot_count // 2, BLK, 2 * BLK)
    half_spec = pl.BlockSpec(half, lambda j: (0, 0, 0), pipeline_mode=pl.Buffered(1))
    return pl.pallas_call(
        functools.partial(grad_kernel, scale),
        grid=(16,),
        out_shape=(jax.ShapeDtypeStruct(half, jnp.bfloat16),) * 2,
        in_specs=[smem] * 4
        + [pl.BlockSpec((1,) + xc.shape[1:], lambda j: (j, 0, 0)), pl.BlockSpec(both.shape, lambda j: (0, 0))],
        out_specs=(half_spec, half_spec),
        scratch_shapes=[pltpu.VMEM((slot_count + 1, BLK, 2 * BLK), jnp.bfloat16)],
        compiler_params=pltpu.CompilerParams(vmem_limit_bytes=14 * MIB),
        cost_estimate=cost,
        name="grad_stage",
    )(*tables, xc, both)


def part_kernel(din_ref, dout_ref, both_ref, *part_refs):
    j = pl.program_id(0)
    tok = both_ref.shape[1] // 2
    win = jnp.concatenate([din_ref[p] for p in range(8)], axis=1)
    wout = jnp.concatenate([dout_ref[p] for p in range(8)], axis=1)
    out = jnp.dot(wout, both_ref[:, tok:], preferred_element_type=jnp.float32).astype(jnp.bfloat16)
    back = jnp.dot(win, both_ref[:, :tok], preferred_element_type=jnp.float32).astype(jnp.bfloat16)
    both = jnp.concatenate([out, back], axis=1)
    for n, ref in enumerate(part_refs):

        @pl.when(j // 2 == n)
        def _():
            ref[...] = both


def part_stage(din, dout, both, quarter, count):
    cost = pl.CostEstimate(
        flops=count * D * 1024 * both.shape[1] // 2, transcendentals=0, bytes_accessed=count * (9 << 19)
    )
    wide = pl.BlockSpec((8, 512, 2 * BLK), lambda j: (0, 2 * quarter + j, 0))
    pieces = tuple(
        pl.BlockSpec((512, both.shape[1]), lambda j, n=n: (jnp.clip(j - 2 * n, 0, 1), 0)) for n in range(count)
    )
    return pl.pallas_call(
        part_kernel,
        grid=(2 * count,),
        out_shape=(jax.ShapeDtypeStruct((1024, both.shape[1]), jnp.bfloat16),) * count,
        in_specs=[wide, wide, pl.BlockSpec(both.shape, lambda j: (0, 0))],
        out_specs=pieces,
        compiler_params=pltpu.CompilerParams(vmem_limit_bytes=16 * MIB),
        cost_estimate=cost,
    )(din, dout, both)


def turn_kernel(own_ref, out_ref, back_ref):
    own = own_ref[...].astype(jnp.float32)
    tok = out_ref.shape[0]
    out_ref[...] = own[:, :tok].T
    back_ref[...] = own[:, tok:].T


def own_turned(own):
    rows, cols = own.shape
    return pl.pallas_call(
        turn_kernel,
        out_shape=(jax.ShapeDtypeStruct((cols // 2, rows), jnp.float32),) * 2,
        compiler_params=pltpu.CompilerParams(vmem_limit_bytes=4 * MIB),
        name="own_turned",
    )(own)


def total_kernel(out_own_ref, back_own_ref, before_ref, after_ref, opposite_ref, out_ref, back_ref):
    refs = (before_ref, after_ref, opposite_ref)
    total = sum(ref[...].astype(jnp.float32) for ref in refs)
    tok = out_ref.shape[0]
    out_ref[...] = (out_own_ref[...] + total[:, :tok].T).astype(jnp.bfloat16)
    back_ref[...] = (back_own_ref[...] + total[:, tok:].T).astype(jnp.bfloat16)


def total_turned(own, terms):
    return pl.pallas_call(
        total_kernel,
        out_shape=tuple(jax.ShapeDtypeStruct(part.shape, jnp.bfloat16) for part in own),
        compiler_params=pltpu.CompilerParams(vmem_limit_bytes=6 * MIB),
        name="total_turned",
    )(*own, *terms)


def ring(axis, stride):
    def target(i, by):
        return i - i // stride % 4 * stride + (i // stride + by) % 4 * stride

    return tuple(
        functools.partial(lax.ppermute, axis_name=axis, perm=[(i, target(i, by)) for i in range(16)])
        for by in (1, 3, 2)
    )


def spread(block, up, down, over):
    return jnp.stack([block, up(block), down(block), over(block)])


def collect(blocks, up, down, over):
    own, before, after, opposite = blocks
    return own, up(after), down(before), over(opposite)


def added(*terms):
    return sum(term.astype(jnp.float32) for term in terms).astype(jnp.bfloat16)


def on_device(tokens, cotangent, block_cols, in_weights, out_weights):
    mp_at, dp_at = lax.axis_index("mp"), lax.axis_index("dp")
    slot_count = in_weights.shape[0]
    tok = tokens.shape[0]
    scale = float(tok * lax.axis_size("dp")) ** (-0.5)
    along_x, along_z, along_y = ring("mp", 4), ring("mp", 1), ring("dp", 2)
    block = jnp.concatenate([tokens, cotangent], axis=0)
    near = spread(block, *along_z)
    tables = slot_tables(block_cols, mp_at, dp_at, slot_count)
    din = dense_weights(tables[0], in_weights, False)
    near, din = lax.optimization_barrier((near, din))
    xc = spread(near, *along_x).reshape(16, 2 * tok, -1)
    dout = dense_weights(tables[0], out_weights, True)
    both = hidden_stage(xc, din, dout, tok)
    (opposite,) = part_stage(din, dout, both, 3, 1)
    opposite, both = lax.optimization_barrier((opposite, both))
    from_opposite = along_x[2](opposite)
    mine, other = grad_stage(tables, xc, both, slot_count, scale)
    other, both = lax.optimization_barrier((other, both))
    from_core = lax.ppermute(other, "dp", [(i, i ^ 1) for i in range(16)])
    own, before, after = part_stage(din, dout, both, 0, 3)
    from_core, _ = lax.optimization_barrier((from_core, before))
    across_terms = own, along_x[0](after), along_x[1](before), from_opposite
    share = slot_count // 8
    pair = [
        added(mine[n * share : (n + 1) * share], from_core[n * share : (n + 1) * share]) for n in range(4)
    ]
    deep_terms = collect(pair, *along_y)
    rows = own.shape[0] // 4
    across = [added(*(term[n * rows : (n + 1) * rows] for term in across_terms)) for n in range(4)]
    deep_terms, _ = lax.optimization_barrier((deep_terms, across[0]))
    half = share // 2
    to_deep = added(*(term[half:] for term in deep_terms))
    from_deep = lax.ppermute(to_deep, "dp", [(i, i ^ 8) for i in range(16)])
    own_part = own_turned(across[0])
    near_terms = collect(across, *along_z)[1:]
    summed = sum(term[:half].astype(jnp.float32) for term in deep_terms) + from_deep.astype(jnp.float32)
    out_grad = summed[:, :, :BLK].reshape(-1, BLK * BLK)
    in_grad = summed[:, :, BLK:].swapaxes(1, 2).reshape(-1, BLK * BLK)
    near_terms, out_grad, in_grad = lax.optimization_barrier((near_terms, out_grad, in_grad))
    layer_out, token_grad = total_turned(own_part, near_terms)
    return (layer_out, token_grad, in_grad, out_grad)


def solution(mesh):
    placed = (P("dp", "mp"), P("dp", "mp"), P(), P("mp", None), P("mp", None))
    return jax.shard_map(
        on_device,
        mesh=mesh,
        in_specs=placed,
        out_specs=(P("dp", "mp"), P("dp", "mp"), P(("mp", "dp"), None), P(("mp", "dp"), None)),
        check_vma=False,
    )
```

```python
import functools

import jax
import jax.numpy as jnp
from jax import lax
from jax.experimental import pallas as pl
from jax.experimental.pallas import tpu as pltpu
from jax.sharding import PartitionSpec as P


D = 4096
BLK = 64
HBL = 16
MIB = 1024 * 1024


def place_of(steps):
    d = steps % 4
    return jnp.where(d == 0, 0, jnp.where(d == 3, 1, jnp.where(d == 1, 2, 3)))


def steps_of(place):
    return jnp.where(place == 0, 0, jnp.where(place == 1, 3, jnp.where(place == 2, 1, 2)))


def slot_tables(block_cols, mp_at, dp_at, slot_count):
    row_count, per_row = block_cols.shape
    flat_cols = block_cols.reshape(1, -1)
    is_mine = flat_cols // HBL == mp_at
    ranks = jnp.cumsum(is_mine.astype(jnp.int32), axis=1, dtype=jnp.int32) - 1
    targets = jnp.where(is_mine, ranks, slot_count)
    row_ids = lax.broadcasted_iota(jnp.int32, flat_cols.shape, 1) // per_row
    packed = row_ids * HBL + flat_cols - mp_at * HBL + 1
    slots = lax.broadcasted_iota(jnp.int32, (slot_count, 1), 0)
    found = jnp.sum(jnp.where(targets == slots, packed, 0), axis=1, dtype=jnp.int32)
    entry = jnp.where(found > 0, found - 1, row_count * HBL)
    place = lax.broadcasted_iota(jnp.int32, (row_count, 1), 0)
    owner = (mp_at // 4 + steps_of(place // 16)) % 4 * 4 + (mp_at % 4 + steps_of(place // 4 % 4)) % 4
    begin = (owner * 4 + place % 4) * HBL
    first = jnp.sum((entry[None, :] < begin).astype(jnp.int32), axis=1, dtype=jnp.int32)
    last = jnp.sum((entry[None, :] < begin + HBL).astype(jnp.int32), axis=1, dtype=jnp.int32)
    row = entry // HBL
    at = place_of(row // 16 - mp_at // 4) * 4 + place_of(row // 4 - mp_at % 4)
    dest = jnp.where(entry < row_count * HBL, (at * 4 + row % 4) * HBL + entry % HBL, row_count * HBL)
    slot = slots[:, 0]
    to = slot // 16
    core, across, deep = (to + dp_at) % 2, place_of(to // 2 - dp_at // 2 % 4), (to // 8 + dp_at // 8) % 2
    late = slot // 8 % 2
    owner_at = jnp.where(late == 0, across * 2 + deep, deep * 4 + across)
    send = ((core * 2 + late) * 8 + owner_at) * 8 + slot % 8
    return dest, send, first, last


def dense_kernel(turned, dest, w_ref, d_ref, lines):
    d_ref[...] = jnp.zeros_like(d_ref)
    at_once = 16
    count = at_once // 2 if turned else at_once
    low = lax.broadcasted_iota(jnp.int32, (count, 2 * BLK), 1) < BLK
    upper = lax.broadcasted_iota(jnp.int32, (BLK, 2 * BLK), 1) >= BLK

    def place(e, block):
        c = e % HBL
        here = d_ref.at[c // 2, pl.ds(pl.multiple_of(e // HBL * BLK, BLK), BLK), :]
        here[...] = jnp.where(upper == (c % 2 == 1), block.astype(jnp.bfloat16), here[...])

    def some(k, carry):
        start = pl.multiple_of(k * at_once, at_once)
        for t in range(BLK // 2):
            two = w_ref[pl.ds(start, at_once), 2 * BLK * t : 2 * BLK * (t + 1)].astype(jnp.float32)
            swapped = pltpu.roll(two, BLK, 1)
            if turned:
                even = jnp.where(low, two[:count], swapped[count:])
                odd = jnp.where(low, swapped[:count], two[count:])
            else:
                even, odd = jnp.where(low, two, swapped), jnp.where(low, swapped, two)
            lines[pl.ds(2 * t, count, stride=BLK), :] = even
            lines[pl.ds(2 * t + 1, count, stride=BLK), :] = odd
        for u in range(count):
            block = lines[u * BLK : (u + 1) * BLK, :]
            if turned:
                both = jnp.concatenate([block, block], axis=0).T
                place(dest[start + u], both[:BLK])
                place(dest[start + u + count], both[BLK:])
            else:
                place(dest[start + u], block)
        return carry

    lax.fori_loop(0, dest.shape[0] // at_once, some, 0)


def dense_weights(dest, weights, turned):
    whole = pl.BlockSpec(memory_space=pltpu.VMEM)
    return pl.pallas_call(
        functools.partial(dense_kernel, turned),
        out_shape=jax.ShapeDtypeStruct((8, D + BLK, 2 * BLK), jnp.bfloat16),
        in_specs=[pl.BlockSpec(memory_space=pltpu.SMEM), whole],
        out_specs=whole,
        scratch_shapes=[pltpu.VMEM((16 * BLK, 2 * BLK), jnp.float32)],
        compiler_params=pltpu.CompilerParams(vmem_limit_bytes=14 * MIB),
        cost_estimate=pl.CostEstimate(flops=0, transcendentals=0, bytes_accessed=20 << 20),
        name="dense_out" if turned else "dense_in",
    )(dest, weights)


def hidden_kernel(xc_ref, din_ref, dout_ref, both_ref):
    tok = xc_ref.shape[1] // 2
    x = jnp.concatenate([xc_ref[j, :tok, :] for j in range(16)], axis=1)
    c = jnp.concatenate([xc_ref[j, tok:, :] for j in range(16)], axis=1)
    win = jnp.concatenate([din_ref[0], din_ref[1]], axis=1)
    wout = jnp.concatenate([dout_ref[0], dout_ref[1]], axis=1)
    v = jnp.dot(x, win, preferred_element_type=jnp.float32)
    g = jnp.dot(c, wout, preferred_element_type=jnp.float32)
    k0 = 0.7978845608028654
    t = jnp.tanh(k0 * (v + 0.044715 * (v * v * v)))
    both_ref[:, tok:] = (0.5 * v * (1.0 + t)).T.astype(jnp.bfloat16)
    slope = 0.5 * (1.0 + t) + 0.5 * v * (1.0 - t * t) * (k0 * (1.0 + 3 * 0.044715 * (v * v)))
    both_ref[:, :tok] = (g * slope).T.astype(jnp.bfloat16)


def hidden_stage(xc, din, dout, tok):
    cost = pl.CostEstimate(flops=4 * tok * D * 1024, transcendentals=tok * 1024, bytes_accessed=18 << 20)
    wide = pl.BlockSpec((2, D, 2 * BLK), lambda q: (q, 0, 0))
    return pl.pallas_call(
        hidden_kernel,
        grid=(4,),
        out_shape=jax.ShapeDtypeStruct((1024, 2 * tok), jnp.bfloat16),
        in_specs=[pl.BlockSpec(xc.shape, lambda q: (0, 0, 0)), wide, wide],
        out_specs=pl.BlockSpec((4 * BLK, 2 * tok), lambda q: (q, 0)),
        compiler_params=pltpu.CompilerParams(vmem_limit_bytes=26 * MIB),
        cost_estimate=cost,
        name="hidden_stage",
    )(xc, din, dout)


def grad_kernel(scale, dest, send, first, last, xc_ref, both_ref, own_ref, other_ref, g_scr):
    j = pl.program_id(0)
    tok = both_ref.shape[1] // 2
    unused = g_scr.shape[0] - 1
    most = 4

    @pl.when(j == 0)
    def _():
        g_scr[...] = jnp.zeros_like(g_scr)

    upper = lax.broadcasted_iota(jnp.int32, (tok, 2 * BLK), 1) >= BLK
    for q in range(4):
        begin, end = first[j * 4 + q], last[j * 4 + q]
        tile = xc_ref[0, :, q // 2 * 2 * BLK : (q // 2 + 1) * 2 * BLK].astype(jnp.float32)
        x, c = tile[:tok], tile[tok:]
        if q % 2:
            c = pltpu.roll(c, BLK, 1)
        else:
            x = pltpu.roll(x, BLK, 1)
        sides = jnp.concatenate([jnp.where(upper, x, 0.0), jnp.where(upper, 0.0, c)], axis=0).astype(jnp.bfloat16)
        blocks, targets = [], []
        for u in range(most):
            s = jnp.minimum(begin + u, unused - 1)
            at = pl.multiple_of(dest[s] % HBL * BLK, BLK)
            blocks.append(both_ref[pl.ds(at, BLK), :])
            targets.append(jnp.where(begin + u < end, send[s], unused))
        terms = jnp.dot(jnp.concatenate(blocks, axis=0), sides, preferred_element_type=jnp.float32)
        terms = (terms * scale).astype(jnp.bfloat16)
        for u in range(most):
            g_scr[targets[u]] = terms[u * BLK : (u + 1) * BLK]

    @pl.when(j == pl.num_programs(0) - 1)
    def _():
        half = own_ref.shape[0]
        own_ref[...] = g_scr[:half]
        other_ref[...] = g_scr[half : 2 * half]


def grad_stage(tables, xc, both, slot_count, scale):
    tok = both.shape[1] // 2
    cost = pl.CostEstimate(flops=tok * D * 1024, transcendentals=0, bytes_accessed=7 << 20)
    smem = pl.BlockSpec(memory_space=pltpu.SMEM)
    half = (slot_count // 2, BLK, 2 * BLK)
    half_spec = pl.BlockSpec(half, lambda j: (0, 0, 0), pipeline_mode=pl.Buffered(1))
    return pl.pallas_call(
        functools.partial(grad_kernel, scale),
        grid=(16,),
        out_shape=(jax.ShapeDtypeStruct(half, jnp.bfloat16),) * 2,
        in_specs=[smem] * 4
        + [pl.BlockSpec((1,) + xc.shape[1:], lambda j: (j, 0, 0)), pl.BlockSpec(both.shape, lambda j: (0, 0))],
        out_specs=(half_spec, half_spec),
        scratch_shapes=[pltpu.VMEM((slot_count + 1, BLK, 2 * BLK), jnp.bfloat16)],
        compiler_params=pltpu.CompilerParams(vmem_limit_bytes=14 * MIB),
        cost_estimate=cost,
        name="grad_stage",
    )(*tables, xc, both)


def part_kernel(din_ref, dout_ref, both_ref, *part_refs):
    j = pl.program_id(0)
    tok = both_ref.shape[1] // 2
    win = jnp.concatenate([din_ref[p] for p in range(8)], axis=1)
    wout = jnp.concatenate([dout_ref[p] for p in range(8)], axis=1)
    out = jnp.dot(wout, both_ref[:, tok:], preferred_element_type=jnp.float32).astype(jnp.bfloat16)
    back = jnp.dot(win, both_ref[:, :tok], preferred_element_type=jnp.float32).astype(jnp.bfloat16)
    both = jnp.concatenate([out, back], axis=1)
    for n, ref in enumerate(part_refs):

        @pl.when(j // 2 == n)
        def _():
            ref[...] = both


def part_stage(din, dout, both, quarter, count):
    cost = pl.CostEstimate(
        flops=count * D * 1024 * both.shape[1] // 2, transcendentals=0, bytes_accessed=count * (9 << 19)
    )
    wide = pl.BlockSpec((8, 512, 2 * BLK), lambda j: (0, 2 * quarter + j, 0))
    pieces = tuple(
        pl.BlockSpec((512, both.shape[1]), lambda j, n=n: (jnp.clip(j - 2 * n, 0, 1), 0)) for n in range(count)
    )
    return pl.pallas_call(
        part_kernel,
        grid=(2 * count,),
        out_shape=(jax.ShapeDtypeStruct((1024, both.shape[1]), jnp.bfloat16),) * count,
        in_specs=[wide, wide, pl.BlockSpec(both.shape, lambda j: (0, 0))],
        out_specs=pieces,
        compiler_params=pltpu.CompilerParams(vmem_limit_bytes=16 * MIB),
        cost_estimate=cost,
    )(din, dout, both)


def turn_kernel(own_ref, out_ref, back_ref):
    own = own_ref[...].astype(jnp.float32)
    tok = out_ref.shape[0]
    out_ref[...] = own[:, :tok].T
    back_ref[...] = own[:, tok:].T


def own_turned(own):
    rows, cols = own.shape
    return pl.pallas_call(
        turn_kernel,
        out_shape=(jax.ShapeDtypeStruct((cols // 2, rows), jnp.float32),) * 2,
        compiler_params=pltpu.CompilerParams(vmem_limit_bytes=4 * MIB),
        name="own_turned",
    )(own)


def total_kernel(out_own_ref, back_own_ref, before_ref, after_ref, opposite_ref, out_ref, back_ref):
    refs = (before_ref, after_ref, opposite_ref)
    total = sum(ref[...].astype(jnp.float32) for ref in refs)
    tok = out_ref.shape[0]
    out_ref[...] = (out_own_ref[...] + total[:, :tok].T).astype(jnp.bfloat16)
    back_ref[...] = (back_own_ref[...] + total[:, tok:].T).astype(jnp.bfloat16)


def total_turned(own, terms):
    return pl.pallas_call(
        total_kernel,
        out_shape=tuple(jax.ShapeDtypeStruct(part.shape, jnp.bfloat16) for part in own),
        compiler_params=pltpu.CompilerParams(vmem_limit_bytes=6 * MIB),
        name="total_turned",
    )(*own, *terms)


def ring(axis, stride):
    def target(i, by):
        return i - i // stride % 4 * stride + (i // stride + by) % 4 * stride

    return tuple(
        functools.partial(lax.ppermute, axis_name=axis, perm=[(i, target(i, by)) for i in range(16)])
        for by in (1, 3, 2)
    )


def sent(block, ways):
    return [way(block) for way in ways]


def collect(blocks, up, down, over):
    own, before, after, opposite = blocks
    return own, up(after), down(before), over(opposite)


def added(*terms):
    return sum(term.astype(jnp.float32) for term in terms).astype(jnp.bfloat16)


def on_device(tokens, cotangent, block_cols, in_weights, out_weights):
    mp_at, dp_at = lax.axis_index("mp"), lax.axis_index("dp")
    slot_count = in_weights.shape[0]
    tok = tokens.shape[0]
    scale = float(tok * lax.axis_size("dp")) ** (-0.5)
    along_x, along_z, along_y = ring("mp", 4), ring("mp", 1), ring("dp", 2)
    block = jnp.concatenate([tokens, cotangent], axis=0)
    near = jnp.stack(sent(block, along_z))
    wide_own = sent(block, along_x)
    tables = slot_tables(block_cols, mp_at, dp_at, slot_count)
    wide = sent(near, along_x)
    pieces = [(own[None], others) for own, others in zip([block] + wide_own, [near] + wide)]
    xc = jnp.concatenate([piece for both in pieces for piece in both])
    dest, _ = lax.optimization_barrier((tables[0], near))
    din = dense_weights(dest, in_weights, False)
    dout = dense_weights(dest, out_weights, True)
    both = hidden_stage(xc, din, dout, tok)
    (opposite,) = part_stage(din, dout, both, 3, 1)
    opposite, both = lax.optimization_barrier((opposite, both))
    from_opposite = along_x[2](opposite)
    mine, other = grad_stage(tables, xc, both, slot_count, scale)
    other, both = lax.optimization_barrier((other, both))
    from_core = lax.ppermute(other, "dp", [(i, i ^ 1) for i in range(16)])
    own, before, after = part_stage(din, dout, both, 0, 3)
    from_core, _ = lax.optimization_barrier((from_core, before))
    across_terms = own, along_x[0](after), along_x[1](before), from_opposite
    share = slot_count // 32
    deep_way = functools.partial(lax.ppermute, axis_name="dp", perm=[(i, i ^ 8) for i in range(16)])

    def pair(at, count):
        return added(mine[at * share : (at + count) * share], from_core[at * share : (at + count) * share])

    late_own, late_other = pair(8, 4), pair(12, 4)
    late_deep = deep_way(late_other)
    deep_terms = collect([pair(2 * n, 2) for n in range(4)], *along_y)
    rows = own.shape[0] // 4
    across = [added(*(term[n * rows : (n + 1) * rows] for term in across_terms)) for n in range(4)]
    deep_terms, late_deep, _ = lax.optimization_barrier((deep_terms, late_deep, across[0]))
    to_deep = added(*(term[share:] for term in deep_terms))
    from_deep = deep_way(to_deep)
    late_terms = collect(
        [
            added(late_own[n * share : (n + 1) * share], late_deep[n * share : (n + 1) * share])
            for n in range(4)
        ],
        *along_y,
    )
    own_part = own_turned(across[0])
    near_terms = collect(across, *along_z)[1:]
    early = sum(term[:share].astype(jnp.float32) for term in deep_terms) + from_deep.astype(jnp.float32)
    late = sum(term.astype(jnp.float32) for term in late_terms)
    summed = jnp.concatenate([early, late])
    out_grad = summed[:, :, :BLK].reshape(-1, BLK * BLK)
    in_grad = summed[:, :, BLK:].swapaxes(1, 2).reshape(-1, BLK * BLK)
    near_terms, out_grad, in_grad = lax.optimization_barrier((near_terms, out_grad, in_grad))
    layer_out, token_grad = total_turned(own_part, near_terms)
    return (layer_out, token_grad, in_grad, out_grad)


def solution(mesh):
    placed = (P("dp", "mp"), P("dp", "mp"), P(), P("mp", None), P("mp", None))
    return jax.shard_map(
        on_device,
        mesh=mesh,
        in_specs=placed,
        out_specs=(P("dp", "mp"), P("dp", "mp"), P(("mp", "dp"), None), P(("mp", "dp"), None)),
        check_vma=False,
    )
```

```python
import functools

import jax
import jax.numpy as jnp
import numpy as np
from jax import lax
from jax.experimental import pallas as pl
from jax.experimental.pallas import tpu as pltpu
from jax.sharding import PartitionSpec as P


D = 4096
BLK = 64
HBL = 16
MIB = 1024 * 1024


def place_of(steps):
    d = steps % 4
    return jnp.where(d == 0, 0, jnp.where(d == 3, 1, jnp.where(d == 1, 2, 3)))


def steps_of(place):
    return jnp.where(place == 0, 0, jnp.where(place == 1, 3, jnp.where(place == 2, 1, 2)))


def slot_tables(block_cols, mp_at, dp_at, slot_count):
    row_count, per_row = block_cols.shape
    flat_cols = block_cols.reshape(1, -1)
    is_mine = flat_cols // HBL == mp_at
    ranks = jnp.cumsum(is_mine.astype(jnp.int32), axis=1, dtype=jnp.int32) - 1
    targets = jnp.where(is_mine, ranks, slot_count)
    row_ids = lax.broadcasted_iota(jnp.int32, flat_cols.shape, 1) // per_row
    packed = row_ids * HBL + flat_cols - mp_at * HBL + 1
    slots = lax.broadcasted_iota(jnp.int32, (slot_count, 1), 0)
    found = jnp.sum(jnp.where(targets == slots, packed, 0), axis=1, dtype=jnp.int32)
    entry = jnp.where(found > 0, found - 1, row_count * HBL)
    place = lax.broadcasted_iota(jnp.int32, (row_count, 1), 0)
    owner = (mp_at // 4 + steps_of(place // 16)) % 4 * 4 + (mp_at % 4 + steps_of(place // 4 % 4)) % 4
    begin = (owner * 4 + place % 4) * HBL
    first = jnp.sum((entry[None, :] < begin).astype(jnp.int32), axis=1, dtype=jnp.int32)
    last = jnp.sum((entry[None, :] < begin + HBL).astype(jnp.int32), axis=1, dtype=jnp.int32)
    row = entry // HBL
    at = place_of(row // 16 - mp_at // 4) * 4 + place_of(row // 4 - mp_at % 4)
    dest = jnp.where(entry < row_count * HBL, (at * 4 + row % 4) * HBL + entry % HBL, row_count * HBL)
    slot = slots[:, 0]
    to = slot // 16
    core, across, deep = (to + dp_at) % 2, place_of(to // 2 - dp_at // 2 % 4), (to // 8 + dp_at // 8) % 2
    late = slot // 8 % 2
    owner_at = jnp.where(late == 0, across * 2 + deep, deep * 4 + across)
    send = ((core * 2 + late) * 8 + owner_at) * 8 + slot % 8
    return dest, send, first, last


def dense_kernel(turned, dest, w_ref, order_ref, d_ref):
    d_ref[...] = jnp.zeros_like(d_ref)
    at_once = 16
    count = 8
    low = lax.broadcasted_iota(jnp.int32, (count, 2 * BLK), 1) < BLK
    upper = lax.broadcasted_iota(jnp.int32, (BLK, 2 * BLK), 1) >= BLK

    def place(e, block):
        here = d_ref.at[(e & (HBL - 1)) >> 1, pl.ds(pl.multiple_of((e >> 4) * BLK, BLK), BLK), :]
        here[...] = jnp.where(upper == ((e & 1) == 1), block.astype(jnp.bfloat16), here[...])

    def lines(even, odd):
        rows = jnp.concatenate(even + odd, axis=0).astype(jnp.bfloat16)
        return jnp.dot(order_ref[...], rows, preferred_element_type=jnp.float32)

    def some(k, carry):
        start = pl.multiple_of(k * at_once, at_once)
        two = [
            w_ref[pl.ds(start, at_once), 2 * BLK * t : 2 * BLK * (t + 1)].astype(jnp.float32)
            for t in range(BLK // 2)
        ]
        swapped = [pltpu.roll(x, BLK, 1) for x in two]
        if turned:
            even = [jnp.where(low, x[:count], y[count:]) for x, y in zip(two, swapped)]
            odd = [jnp.where(low, y[:count], x[count:]) for x, y in zip(two, swapped)]
            blocks = lines(even, odd)
            for u in range(count):
                block = blocks[u * BLK : (u + 1) * BLK]
                both = jnp.concatenate([block, block], axis=0).T
                place(dest[start + u], both[:BLK])
                place(dest[start + u + count], both[BLK:])
        else:
            for half in range(2):
                part = slice(half * count, (half + 1) * count)
                even = [jnp.where(low, x[part], y[part]) for x, y in zip(two, swapped)]
                odd = [jnp.where(low, y[part], x[part]) for x, y in zip(two, swapped)]
                blocks = lines(even, odd)
                for u in range(count):
                    place(dest[start + half * count + u], blocks[u * BLK : (u + 1) * BLK])
        return carry

    lax.fori_loop(0, dest.shape[0] // at_once, some, 0)


def line_order():
    to, at = np.indices((8 * BLK, 8 * BLK))
    row = at // 8 % (BLK // 2) * 2 + at // (4 * BLK)
    return jnp.asarray((to == at % 8 * BLK + row).astype(jnp.bfloat16))


def dense_weights(dest, weights, order, turned):
    whole = pl.BlockSpec(memory_space=pltpu.VMEM)
    return pl.pallas_call(
        functools.partial(dense_kernel, turned),
        out_shape=jax.ShapeDtypeStruct((8, D + BLK, 2 * BLK), jnp.bfloat16),
        in_specs=[pl.BlockSpec(memory_space=pltpu.SMEM), whole, whole],
        out_specs=whole,
        compiler_params=pltpu.CompilerParams(vmem_limit_bytes=15 * MIB),
        cost_estimate=pl.CostEstimate(flops=0, transcendentals=0, bytes_accessed=20 << 20),
        name="dense_out" if turned else "dense_in",
    )(dest, weights, order)


def hidden_kernel(xc_ref, din_ref, dout_ref, both_ref):
    tok = xc_ref.shape[1] // 2
    x = jnp.concatenate([xc_ref[j, :tok, :] for j in range(16)], axis=1)
    c = jnp.concatenate([xc_ref[j, tok:, :] for j in range(16)], axis=1)

    def some(q, carry):
        win = jnp.concatenate([din_ref[2 * q + p, :D] for p in range(2)], axis=1)
        wout = jnp.concatenate([dout_ref[2 * q + p, :D] for p in range(2)], axis=1)
        v = jnp.dot(x, win, preferred_element_type=jnp.float32)
        g = jnp.dot(c, wout, preferred_element_type=jnp.float32)
        k0 = 0.7978845608028654
        t = jnp.tanh(k0 * (v + 0.044715 * (v * v * v)))
        rows = pl.ds(pl.multiple_of(q * 4 * BLK, 4 * BLK), 4 * BLK)
        both_ref[rows, tok:] = (0.5 * v * (1.0 + t)).T.astype(jnp.bfloat16)
        slope = 0.5 * (1.0 + t) + 0.5 * v * (1.0 - t * t) * (k0 * (1.0 + 3 * 0.044715 * (v * v)))
        both_ref[rows, :tok] = (g * slope).T.astype(jnp.bfloat16)
        return carry

    lax.fori_loop(0, 4, some, 0)


def hidden_stage(xc, din, dout, tok):
    cost = pl.CostEstimate(flops=4 * tok * D * 1024, transcendentals=tok * 1024, bytes_accessed=18 << 20)
    whole = pl.BlockSpec(memory_space=pltpu.VMEM)
    return pl.pallas_call(
        hidden_kernel,
        out_shape=jax.ShapeDtypeStruct((1024, 2 * tok), jnp.bfloat16),
        in_specs=[whole] * 3,
        out_specs=whole,
        compiler_params=pltpu.CompilerParams(vmem_limit_bytes=26 * MIB),
        cost_estimate=cost,
        name="hidden_stage",
    )(xc, din, dout)


def grad_kernel(scale, dest, send, first, last, xc_ref, both_ref, own_ref, other_ref, g_scr):
    j = pl.program_id(0)
    tok = both_ref.shape[1] // 2
    unused = g_scr.shape[0] - 1
    most = 4

    @pl.when(j == 0)
    def _():
        g_scr[...] = jnp.zeros_like(g_scr)

    upper = lax.broadcasted_iota(jnp.int32, (tok, 2 * BLK), 1) >= BLK
    for q in range(4):
        begin, end = first[j * 4 + q], last[j * 4 + q]
        tile = xc_ref[0, :, q // 2 * 2 * BLK : (q // 2 + 1) * 2 * BLK].astype(jnp.float32)
        x, c = tile[:tok], tile[tok:]
        if q % 2:
            c = pltpu.roll(c, BLK, 1)
        else:
            x = pltpu.roll(x, BLK, 1)
        sides = jnp.concatenate([jnp.where(upper, x, 0.0), jnp.where(upper, 0.0, c)], axis=0).astype(jnp.bfloat16)
        blocks, targets = [], []
        for u in range(most):
            s = jnp.minimum(begin + u, unused - 1)
            at = pl.multiple_of((dest[s] & (HBL - 1)) * BLK, BLK)
            blocks.append(both_ref[pl.ds(at, BLK), :])
            targets.append(jnp.where(begin + u < end, send[s], unused))
        terms = jnp.dot(jnp.concatenate(blocks, axis=0), sides, preferred_element_type=jnp.float32)
        terms = (terms * scale).astype(jnp.bfloat16)
        for u in range(most):
            g_scr[targets[u]] = terms[u * BLK : (u + 1) * BLK]

    @pl.when(j == pl.num_programs(0) - 1)
    def _():
        half = own_ref.shape[0]
        own_ref[...] = g_scr[:half]
        other_ref[...] = g_scr[half : 2 * half]


def grad_stage(tables, xc, both, slot_count, scale):
    tok = both.shape[1] // 2
    cost = pl.CostEstimate(flops=tok * D * 1024, transcendentals=0, bytes_accessed=7 << 20)
    smem = pl.BlockSpec(memory_space=pltpu.SMEM)
    half = (slot_count // 2, BLK, 2 * BLK)
    half_spec = pl.BlockSpec(half, lambda j: (0, 0, 0), pipeline_mode=pl.Buffered(1))
    return pl.pallas_call(
        functools.partial(grad_kernel, scale),
        grid=(16,),
        out_shape=(jax.ShapeDtypeStruct(half, jnp.bfloat16),) * 2,
        in_specs=[smem] * 4
        + [pl.BlockSpec((1,) + xc.shape[1:], lambda j: (j, 0, 0)), pl.BlockSpec(both.shape, lambda j: (0, 0))],
        out_specs=(half_spec, half_spec),
        scratch_shapes=[pltpu.VMEM((slot_count + 1, BLK, 2 * BLK), jnp.bfloat16)],
        compiler_params=pltpu.CompilerParams(vmem_limit_bytes=14 * MIB),
        cost_estimate=cost,
        name="grad_stage",
    )(*tables, xc, both)


def part_kernel(quarter, din_ref, dout_ref, both_ref, *part_refs):
    tok = both_ref.shape[1] // 2
    size = 512
    for n, ref in enumerate(part_refs):

        def some(j, carry):
            rows = pl.ds(pl.multiple_of((quarter + n) * 1024 + j * size, size), size)
            win = jnp.concatenate([din_ref[p, rows, :] for p in range(8)], axis=1)
            wout = jnp.concatenate([dout_ref[p, rows, :] for p in range(8)], axis=1)
            out = jnp.dot(wout, both_ref[:, tok:], preferred_element_type=jnp.float32)
            back = jnp.dot(win, both_ref[:, :tok], preferred_element_type=jnp.float32)
            to = pl.ds(pl.multiple_of(j * size, size), size)
            ref[to, :] = jnp.concatenate([out, back], axis=1).astype(jnp.bfloat16)
            return carry

        lax.fori_loop(0, 1024 // size, some, 0)


def part_stage(din, dout, both, quarter, count):
    cost = pl.CostEstimate(
        flops=count * D * 1024 * both.shape[1] // 2, transcendentals=0, bytes_accessed=count * (9 << 19)
    )
    whole = pl.BlockSpec(memory_space=pltpu.VMEM)
    return pl.pallas_call(
        functools.partial(part_kernel, quarter),
        out_shape=(jax.ShapeDtypeStruct((1024, both.shape[1]), jnp.bfloat16),) * count,
        in_specs=[whole] * 3,
        out_specs=(whole,) * count,
        compiler_params=pltpu.CompilerParams(vmem_limit_bytes=24 * MIB),
        cost_estimate=cost,
    )(din, dout, both)


def turn_kernel(own_ref, out_ref, back_ref):
    own = own_ref[...].astype(jnp.float32)
    tok = out_ref.shape[0]
    out_ref[...] = own[:, :tok].T
    back_ref[...] = own[:, tok:].T


def own_turned(own):
    rows, cols = own.shape
    return pl.pallas_call(
        turn_kernel,
        out_shape=(jax.ShapeDtypeStruct((cols // 2, rows), jnp.float32),) * 2,
        compiler_params=pltpu.CompilerParams(vmem_limit_bytes=4 * MIB),
        name="own_turned",
    )(own)


def total_kernel(out_own_ref, back_own_ref, before_ref, after_ref, opposite_ref, out_ref, back_ref):
    refs = (before_ref, after_ref, opposite_ref)
    total = sum(ref[...].astype(jnp.float32) for ref in refs)
    tok = out_ref.shape[0]
    out_ref[...] = (out_own_ref[...] + total[:, :tok].T).astype(jnp.bfloat16)
    back_ref[...] = (back_own_ref[...] + total[:, tok:].T).astype(jnp.bfloat16)


def total_turned(own, terms):
    return pl.pallas_call(
        total_kernel,
        out_shape=tuple(jax.ShapeDtypeStruct(part.shape, jnp.bfloat16) for part in own),
        compiler_params=pltpu.CompilerParams(vmem_limit_bytes=6 * MIB),
        name="total_turned",
    )(*own, *terms)


def ring(axis, stride):
    def target(i, by):
        return i - i // stride % 4 * stride + (i // stride + by) % 4 * stride

    return tuple(
        functools.partial(lax.ppermute, axis_name=axis, perm=[(i, target(i, by)) for i in range(16)])
        for by in (1, 3, 2)
    )


def sent(block, ways):
    return [way(block) for way in ways]


def collect(blocks, up, down, over):
    own, before, after, opposite = blocks
    return own, up(after), down(before), over(opposite)


def added(*terms):
    return sum(term.astype(jnp.float32) for term in terms).astype(jnp.bfloat16)


def on_device(tokens, cotangent, block_cols, in_weights, out_weights):
    mp_at, dp_at = lax.axis_index("mp"), lax.axis_index("dp")
    slot_count = in_weights.shape[0]
    tok = tokens.shape[0]
    scale = float(tok * lax.axis_size("dp")) ** (-0.5)
    along_x, along_z, along_y = ring("mp", 4), ring("mp", 1), ring("dp", 2)
    block = jnp.concatenate([tokens, cotangent], axis=0)
    near = jnp.stack(sent(block, along_z))
    wide_own = sent(block, along_x)
    tables = slot_tables(block_cols, mp_at, dp_at, slot_count)
    wide = sent(near, along_x)
    pieces = [(own[None], others) for own, others in zip([block] + wide_own, [near] + wide)]
    xc = jnp.concatenate([piece for both in pieces for piece in both])
    order = line_order()
    dest, _ = lax.optimization_barrier((tables[0], near))
    din = dense_weights(dest, in_weights, order, False)
    dout = dense_weights(dest, out_weights, order, True)
    both = hidden_stage(xc, din, dout, tok)
    (opposite,) = part_stage(din, dout, both, 3, 1)
    opposite, both = lax.optimization_barrier((opposite, both))
    from_opposite = along_x[2](opposite)
    mine, other = grad_stage(tables, xc, both, slot_count, scale)
    other, both = lax.optimization_barrier((other, both))
    from_core = lax.ppermute(other, "dp", [(i, i ^ 1) for i in range(16)])
    own, before, after = part_stage(din, dout, both, 0, 3)
    from_core, _ = lax.optimization_barrier((from_core, before))
    across_terms = own, along_x[0](after), along_x[1](before), from_opposite
    share = slot_count // 32
    deep_way = functools.partial(lax.ppermute, axis_name="dp", perm=[(i, i ^ 8) for i in range(16)])

    def pair(at, count):
        return added(mine[at * share : (at + count) * share], from_core[at * share : (at + count) * share])

    late_own, late_other = pair(8, 4), pair(12, 4)
    late_deep = deep_way(late_other)
    deep_terms = collect([pair(2 * n, 2) for n in range(4)], *along_y)
    rows = own.shape[0] // 4
    across = [added(*(term[n * rows : (n + 1) * rows] for term in across_terms)) for n in range(4)]
    deep_terms, late_deep, _ = lax.optimization_barrier((deep_terms, late_deep, across[0]))
    to_deep = added(*(term[share:] for term in deep_terms))
    from_deep = deep_way(to_deep)
    late_terms = collect(
        [
            added(late_own[n * share : (n + 1) * share], late_deep[n * share : (n + 1) * share])
            for n in range(4)
        ],
        *along_y,
    )
    own_part = own_turned(across[0])
    near_terms = collect(across, *along_z)[1:]
    early = sum(term[:share].astype(jnp.float32) for term in deep_terms) + from_deep.astype(jnp.float32)
    late = sum(term.astype(jnp.float32) for term in late_terms)
    summed = jnp.concatenate([early, late])
    out_grad = summed[:, :, :BLK].reshape(-1, BLK * BLK)
    in_grad = summed[:, :, BLK:].swapaxes(1, 2).reshape(-1, BLK * BLK)
    near_terms, out_grad, in_grad = lax.optimization_barrier((near_terms, out_grad, in_grad))
    layer_out, token_grad = total_turned(own_part, near_terms)
    return (layer_out, token_grad, in_grad, out_grad)


def solution(mesh):
    placed = (P("dp", "mp"), P("dp", "mp"), P(), P("mp", None), P("mp", None))
    return jax.shard_map(
        on_device,
        mesh=mesh,
        in_specs=placed,
        out_specs=(P("dp", "mp"), P("dp", "mp"), P(("mp", "dp"), None), P(("mp", "dp"), None)),
        check_vma=False,
    )
```

```python
import functools

import jax
import jax.numpy as jnp
from jax import lax
from jax.experimental import pallas as pl
from jax.experimental.pallas import tpu as pltpu
from jax.sharding import PartitionSpec as P


D = 4096
BLK = 64
HBL = 16
MIB = 1024 * 1024


def place_of(steps):
    d = steps % 4
    return jnp.where(d == 0, 0, jnp.where(d == 3, 1, jnp.where(d == 1, 2, 3)))


def steps_of(place):
    return jnp.where(place == 0, 0, jnp.where(place == 1, 3, jnp.where(place == 2, 1, 2)))


def slot_tables(block_cols, mp_at, dp_at, slot_count):
    row_count, per_row = block_cols.shape
    flat_cols = block_cols.reshape(1, -1)
    is_mine = flat_cols // HBL == mp_at
    ranks = jnp.cumsum(is_mine.astype(jnp.int32), axis=1, dtype=jnp.int32) - 1
    targets = jnp.where(is_mine, ranks, slot_count)
    row_ids = lax.broadcasted_iota(jnp.int32, flat_cols.shape, 1) // per_row
    packed = row_ids * HBL + flat_cols - mp_at * HBL + 1
    slots = lax.broadcasted_iota(jnp.int32, (slot_count, 1), 0)
    found = jnp.sum(jnp.where(targets == slots, packed, 0), axis=1, dtype=jnp.int32)
    entry = jnp.where(found > 0, found - 1, row_count * HBL)
    place = lax.broadcasted_iota(jnp.int32, (row_count, 1), 0)
    owner = (mp_at // 4 + steps_of(place // 16)) % 4 * 4 + (mp_at % 4 + steps_of(place // 4 % 4)) % 4
    begin = (owner * 4 + place % 4) * HBL
    first = jnp.sum((entry[None, :] < begin).astype(jnp.int32), axis=1, dtype=jnp.int32)
    last = jnp.sum((entry[None, :] < begin + HBL).astype(jnp.int32), axis=1, dtype=jnp.int32)
    row = entry // HBL
    at = place_of(row // 16 - mp_at // 4) * 4 + place_of(row // 4 - mp_at % 4)
    dest = jnp.where(entry < row_count * HBL, (at * 4 + row % 4) * HBL + entry % HBL, row_count * HBL)
    slot = slots[:, 0]
    to = slot // 16
    core, across, deep = (to + dp_at) % 2, place_of(to // 2 - dp_at // 2 % 4), (to // 8 + dp_at // 8) % 2
    late = slot // 8 % 2
    owner_at = jnp.where(late == 0, across * 2 + deep, deep * 4 + across)
    send = ((core * 2 + late) * 8 + owner_at) * 8 + slot % 8
    return dest, send, first, last


def dense_kernel(turned, dest, w_ref, d_ref, lines):
    d_ref[...] = jnp.zeros_like(d_ref)
    at_once = 16
    count = at_once // 2 if turned else at_once
    low = lax.broadcasted_iota(jnp.int32, (count, 2 * BLK), 1) < BLK
    upper = lax.broadcasted_iota(jnp.int32, (BLK, 2 * BLK), 1) >= BLK

    def place(e, block):
        here = d_ref.at[(e & (HBL - 1)) >> 1, pl.ds(pl.multiple_of((e >> 4) * BLK, BLK), BLK), :]
        here[...] = jnp.where(upper == ((e & 1) == 1), block.astype(jnp.bfloat16), here[...])

    def some(k, carry):
        start = pl.multiple_of(k * at_once, at_once)
        for t in range(BLK // 2):
            two = w_ref[pl.ds(start, at_once), 2 * BLK * t : 2 * BLK * (t + 1)].astype(jnp.float32)
            swapped = pltpu.roll(two, BLK, 1)
            if turned:
                even = jnp.where(low, two[:count], swapped[count:])
                odd = jnp.where(low, swapped[:count], two[count:])
            else:
                even, odd = jnp.where(low, two, swapped), jnp.where(low, swapped, two)
            lines[pl.ds(2 * t, count, stride=BLK), :] = even
            lines[pl.ds(2 * t + 1, count, stride=BLK), :] = odd
        for u in range(count):
            block = lines[u * BLK : (u + 1) * BLK, :]
            if turned:
                both = jnp.concatenate([block, block], axis=0).T
                place(dest[start + u], both[:BLK])
                place(dest[start + u + count], both[BLK:])
            else:
                place(dest[start + u], block)
        return carry

    lax.fori_loop(0, dest.shape[0] // at_once, some, 0)


def dense_weights(dest, weights, turned):
    whole = pl.BlockSpec(memory_space=pltpu.VMEM)
    return pl.pallas_call(
        functools.partial(dense_kernel, turned),
        out_shape=jax.ShapeDtypeStruct((8, D + BLK, 2 * BLK), jnp.bfloat16),
        in_specs=[pl.BlockSpec(memory_space=pltpu.SMEM), whole],
        out_specs=whole,
        scratch_shapes=[pltpu.VMEM((16 * BLK, 2 * BLK), jnp.float32)],
        compiler_params=pltpu.CompilerParams(vmem_limit_bytes=14 * MIB),
        cost_estimate=pl.CostEstimate(flops=0, transcendentals=0, bytes_accessed=20 << 20),
        name="dense_out" if turned else "dense_in",
    )(dest, weights)


def hidden_kernel(xc_ref, din_ref, dout_ref, both_ref):
    tok = xc_ref.shape[1] // 2
    x = jnp.concatenate([xc_ref[j, :tok, :] for j in range(16)], axis=1)
    c = jnp.concatenate([xc_ref[j, tok:, :] for j in range(16)], axis=1)

    def some(q, carry):
        win = jnp.concatenate([din_ref[2 * q + p, :D] for p in range(2)], axis=1)
        wout = jnp.concatenate([dout_ref[2 * q + p, :D] for p in range(2)], axis=1)
        v = jnp.dot(x, win, preferred_element_type=jnp.float32)
        g = jnp.dot(c, wout, preferred_element_type=jnp.float32)
        k0 = 0.7978845608028654
        t = jnp.tanh(k0 * (v + 0.044715 * (v * v * v)))
        rows = pl.ds(pl.multiple_of(q * 4 * BLK, 4 * BLK), 4 * BLK)
        both_ref[rows, tok:] = (0.5 * v * (1.0 + t)).T.astype(jnp.bfloat16)
        slope = 0.5 * (1.0 + t) + 0.5 * v * (1.0 - t * t) * (k0 * (1.0 + 3 * 0.044715 * (v * v)))
        both_ref[rows, :tok] = (g * slope).T.astype(jnp.bfloat16)
        return carry

    lax.fori_loop(0, 4, some, 0)


def hidden_stage(xc, din, dout, tok):
    cost = pl.CostEstimate(flops=4 * tok * D * 1024, transcendentals=tok * 1024, bytes_accessed=18 << 20)
    whole = pl.BlockSpec(memory_space=pltpu.VMEM)
    return pl.pallas_call(
        hidden_kernel,
        out_shape=jax.ShapeDtypeStruct((1024, 2 * tok), jnp.bfloat16),
        in_specs=[whole] * 3,
        out_specs=whole,
        compiler_params=pltpu.CompilerParams(vmem_limit_bytes=16 * MIB),
        cost_estimate=cost,
        name="hidden_stage",
    )(xc, din, dout)


def grad_kernel(scale, dest, send, first, last, xc_ref, both_ref, own_ref, other_ref, g_scr):
    j = pl.program_id(0)
    tok = both_ref.shape[1] // 2
    unused = g_scr.shape[0] - 1
    most = 4

    @pl.when(j == 0)
    def _():
        g_scr[...] = jnp.zeros_like(g_scr)

    upper = lax.broadcasted_iota(jnp.int32, (tok, 2 * BLK), 1) >= BLK
    for q in range(4):
        begin, end = first[j * 4 + q], last[j * 4 + q]
        tile = xc_ref[0, :, q // 2 * 2 * BLK : (q // 2 + 1) * 2 * BLK].astype(jnp.float32)
        x, c = tile[:tok], tile[tok:]
        if q % 2:
            c = pltpu.roll(c, BLK, 1)
        else:
            x = pltpu.roll(x, BLK, 1)
        sides = jnp.concatenate([jnp.where(upper, x, 0.0), jnp.where(upper, 0.0, c)], axis=0).astype(jnp.bfloat16)
        blocks, targets = [], []
        for u in range(most):
            s = jnp.minimum(begin + u, unused - 1)
            at = pl.multiple_of((dest[s] & (HBL - 1)) * BLK, BLK)
            blocks.append(both_ref[pl.ds(at, BLK), :])
            targets.append(jnp.where(begin + u < end, send[s], unused))
        terms = jnp.dot(jnp.concatenate(blocks, axis=0), sides, preferred_element_type=jnp.float32)
        terms = (terms * scale).astype(jnp.bfloat16)
        for u in range(most):
            g_scr[targets[u]] = terms[u * BLK : (u + 1) * BLK]

    @pl.when(j == pl.num_programs(0) - 1)
    def _():
        half = own_ref.shape[0]
        own_ref[...] = g_scr[:half]
        other_ref[...] = g_scr[half : 2 * half]


def grad_stage(tables, xc, both, slot_count, scale):
    tok = both.shape[1] // 2
    cost = pl.CostEstimate(flops=tok * D * 1024, transcendentals=0, bytes_accessed=7 << 20)
    smem = pl.BlockSpec(memory_space=pltpu.SMEM)
    half = (slot_count // 2, BLK, 2 * BLK)
    half_spec = pl.BlockSpec(half, lambda j: (0, 0, 0), pipeline_mode=pl.Buffered(1))
    return pl.pallas_call(
        functools.partial(grad_kernel, scale),
        grid=(16,),
        out_shape=(jax.ShapeDtypeStruct(half, jnp.bfloat16),) * 2,
        in_specs=[smem] * 4
        + [pl.BlockSpec((1,) + xc.shape[1:], lambda j: (j, 0, 0)), pl.BlockSpec(both.shape, lambda j: (0, 0))],
        out_specs=(half_spec, half_spec),
        scratch_shapes=[pltpu.VMEM((slot_count + 1, BLK, 2 * BLK), jnp.bfloat16)],
        compiler_params=pltpu.CompilerParams(vmem_limit_bytes=14 * MIB),
        cost_estimate=cost,
        name="grad_stage",
    )(*tables, xc, both)


def part_kernel(quarter, din_ref, dout_ref, both_ref, *part_refs):
    tok = both_ref.shape[1] // 2
    size = 512
    for n, ref in enumerate(part_refs):

        def some(j, carry):
            rows = pl.ds(pl.multiple_of((quarter + n) * 1024 + j * size, size), size)
            win = jnp.concatenate([din_ref[p, rows, :] for p in range(8)], axis=1)
            wout = jnp.concatenate([dout_ref[p, rows, :] for p in range(8)], axis=1)
            out = jnp.dot(wout, both_ref[:, tok:], preferred_element_type=jnp.float32)
            back = jnp.dot(win, both_ref[:, :tok], preferred_element_type=jnp.float32)
            to = pl.ds(pl.multiple_of(j * size, size), size)
            ref[to, :] = jnp.concatenate([out, back], axis=1).astype(jnp.bfloat16)
            return carry

        lax.fori_loop(0, 1024 // size, some, 0)


def part_stage(din, dout, both, quarter, count):
    cost = pl.CostEstimate(
        flops=count * D * 1024 * both.shape[1] // 2, transcendentals=0, bytes_accessed=count * (9 << 19)
    )
    whole = pl.BlockSpec(memory_space=pltpu.VMEM)
    return pl.pallas_call(
        functools.partial(part_kernel, quarter),
        out_shape=(jax.ShapeDtypeStruct((1024, both.shape[1]), jnp.bfloat16),) * count,
        in_specs=[whole] * 3,
        out_specs=(whole,) * count,
        compiler_params=pltpu.CompilerParams(vmem_limit_bytes=12 * MIB),
        cost_estimate=cost,
    )(din, dout, both)


def turn_kernel(own_ref, out_ref, back_ref):
    own = own_ref[...].astype(jnp.float32)
    tok = out_ref.shape[0]
    out_ref[...] = own[:, :tok].T
    back_ref[...] = own[:, tok:].T


def own_turned(own):
    rows, cols = own.shape
    return pl.pallas_call(
        turn_kernel,
        out_shape=(jax.ShapeDtypeStruct((cols // 2, rows), jnp.float32),) * 2,
        compiler_params=pltpu.CompilerParams(vmem_limit_bytes=4 * MIB),
        name="own_turned",
    )(own)


def total_kernel(out_own_ref, back_own_ref, before_ref, after_ref, opposite_ref, out_ref, back_ref):
    refs = (before_ref, after_ref, opposite_ref)
    total = sum(ref[...].astype(jnp.float32) for ref in refs)
    tok = out_ref.shape[0]
    out_ref[...] = (out_own_ref[...] + total[:, :tok].T).astype(jnp.bfloat16)
    back_ref[...] = (back_own_ref[...] + total[:, tok:].T).astype(jnp.bfloat16)


def total_turned(own, terms):
    return pl.pallas_call(
        total_kernel,
        out_shape=tuple(jax.ShapeDtypeStruct(part.shape, jnp.bfloat16) for part in own),
        compiler_params=pltpu.CompilerParams(vmem_limit_bytes=6 * MIB),
        name="total_turned",
    )(*own, *terms)


def ring(axis, stride):
    def target(i, by):
        return i - i // stride % 4 * stride + (i // stride + by) % 4 * stride

    return tuple(
        functools.partial(lax.ppermute, axis_name=axis, perm=[(i, target(i, by)) for i in range(16)])
        for by in (1, 3, 2)
    )


def sent(block, ways):
    return [way(block) for way in ways]


def collect(blocks, up, down, over):
    own, before, after, opposite = blocks
    return own, up(after), down(before), over(opposite)


def added(*terms):
    return sum(term.astype(jnp.float32) for term in terms).astype(jnp.bfloat16)


def on_device(tokens, cotangent, block_cols, in_weights, out_weights):
    mp_at, dp_at = lax.axis_index("mp"), lax.axis_index("dp")
    slot_count = in_weights.shape[0]
    tok = tokens.shape[0]
    scale = float(tok * lax.axis_size("dp")) ** (-0.5)
    along_x, along_z, along_y = ring("mp", 4), ring("mp", 1), ring("dp", 2)
    block = jnp.concatenate([tokens, cotangent], axis=0)
    near = jnp.stack(sent(block, along_z))
    wide_own = sent(block, along_x)
    tables = slot_tables(block_cols, mp_at, dp_at, slot_count)
    wide = sent(near, along_x)
    pieces = [(own[None], others) for own, others in zip([block] + wide_own, [near] + wide)]
    xc = jnp.concatenate([piece for both in pieces for piece in both])
    dest, _ = lax.optimization_barrier((tables[0], near))
    din = dense_weights(dest, in_weights, False)
    dout = dense_weights(dest, out_weights, True)
    both = hidden_stage(xc, din, dout, tok)
    (opposite,) = part_stage(din, dout, both, 3, 1)
    opposite, both = lax.optimization_barrier((opposite, both))
    from_opposite = along_x[2](opposite)
    mine, other = grad_stage(tables, xc, both, slot_count, scale)
    other, both = lax.optimization_barrier((other, both))
    from_core = lax.ppermute(other, "dp", [(i, i ^ 1) for i in range(16)])
    own, before, after = part_stage(din, dout, both, 0, 3)
    from_core, _ = lax.optimization_barrier((from_core, before))
    across_terms = own, along_x[0](after), along_x[1](before), from_opposite
    share = slot_count // 32
    deep_way = functools.partial(lax.ppermute, axis_name="dp", perm=[(i, i ^ 8) for i in range(16)])

    def pair(at, count):
        return added(mine[at * share : (at + count) * share], from_core[at * share : (at + count) * share])

    late_own, late_other = pair(8, 4), pair(12, 4)
    late_deep = deep_way(late_other)
    deep_terms = collect([pair(2 * n, 2) for n in range(4)], *along_y)
    rows = own.shape[0] // 4
    across = [added(*(term[n * rows : (n + 1) * rows] for term in across_terms)) for n in range(4)]
    deep_terms, late_deep, _ = lax.optimization_barrier((deep_terms, late_deep, across[0]))
    to_deep = added(*(term[share:] for term in deep_terms))
    from_deep = deep_way(to_deep)
    late_terms = collect(
        [
            added(late_own[n * share : (n + 1) * share], late_deep[n * share : (n + 1) * share])
            for n in range(4)
        ],
        *along_y,
    )
    own_part = own_turned(across[0])
    near_terms = collect(across, *along_z)[1:]
    early = sum(term[:share].astype(jnp.float32) for term in deep_terms) + from_deep.astype(jnp.float32)
    late = sum(term.astype(jnp.float32) for term in late_terms)
    summed = jnp.concatenate([early, late])
    out_grad = summed[:, :, :BLK].reshape(-1, BLK * BLK)
    in_grad = summed[:, :, BLK:].swapaxes(1, 2).reshape(-1, BLK * BLK)
    near_terms, out_grad, in_grad = lax.optimization_barrier((near_terms, out_grad, in_grad))
    layer_out, token_grad = total_turned(own_part, near_terms)
    return (layer_out, token_grad, in_grad, out_grad)


def solution(mesh):
    placed = (P("dp", "mp"), P("dp", "mp"), P(), P("mp", None), P("mp", None))
    return jax.shard_map(
        on_device,
        mesh=mesh,
        in_specs=placed,
        out_specs=(P("dp", "mp"), P("dp", "mp"), P(("mp", "dp"), None), P(("mp", "dp"), None)),
        check_vma=False,
    )
```

```python
import functools

import jax
import jax.numpy as jnp
from jax import lax
from jax.experimental import pallas as pl
from jax.experimental.pallas import tpu as pltpu
from jax.sharding import PartitionSpec as P


D = 4096
BLK = 64
HBL = 16
MIB = 1024 * 1024


def place_of(steps):
    d = steps % 4
    return jnp.where(d == 0, 0, jnp.where(d == 3, 1, jnp.where(d == 1, 2, 3)))


def steps_of(place):
    return jnp.where(place == 0, 0, jnp.where(place == 1, 3, jnp.where(place == 2, 1, 2)))


def slot_tables(block_cols, mp_at, dp_at, slot_count):
    row_count, per_row = block_cols.shape
    flat_cols = block_cols.reshape(1, -1)
    is_mine = flat_cols // HBL == mp_at
    ranks = jnp.cumsum(is_mine.astype(jnp.int32), axis=1, dtype=jnp.int32) - 1
    targets = jnp.where(is_mine, ranks, slot_count)
    row_ids = lax.broadcasted_iota(jnp.int32, flat_cols.shape, 1) // per_row
    packed = row_ids * HBL + flat_cols - mp_at * HBL + 1
    slots = lax.broadcasted_iota(jnp.int32, (slot_count, 1), 0)
    found = jnp.sum(jnp.where(targets == slots, packed, 0), axis=1, dtype=jnp.int32)
    entry = jnp.where(found > 0, found - 1, row_count * HBL)
    place = lax.broadcasted_iota(jnp.int32, (row_count, 1), 0)
    owner = (mp_at // 4 + steps_of(place // 16)) % 4 * 4 + (mp_at % 4 + steps_of(place // 4 % 4)) % 4
    begin = (owner * 4 + place % 4) * HBL
    first = jnp.sum((entry[None, :] < begin).astype(jnp.int32), axis=1, dtype=jnp.int32)
    last = jnp.sum((entry[None, :] < begin + HBL).astype(jnp.int32), axis=1, dtype=jnp.int32)
    row = entry // HBL
    at = place_of(row // 16 - mp_at // 4) * 4 + place_of(row // 4 - mp_at % 4)
    dest = jnp.where(entry < row_count * HBL, (at * 4 + row % 4) * HBL + entry % HBL, row_count * HBL)
    slot = slots[:, 0]
    to = slot // 16
    core, across, deep = (to + dp_at) % 2, place_of(to // 2 - dp_at // 2 % 4), (to // 8 + dp_at // 8) % 2
    late = slot // 8 % 2
    owner_at = jnp.where(late == 0, across * 2 + deep, deep * 4 + across)
    send = ((core * 2 + late) * 8 + owner_at) * 8 + slot % 8
    return dest, send, first, last


def dense_kernel(turned, dest, w_ref, d_ref, lines):
    d_ref[...] = jnp.zeros_like(d_ref)
    at_once = 16
    count = at_once // 2 if turned else at_once
    low = lax.broadcasted_iota(jnp.int32, (count, 2 * BLK), 1) < BLK
    upper = lax.broadcasted_iota(jnp.int32, (BLK, 2 * BLK), 1) >= BLK

    def place(blocks):
        placed = []
        for e, block in blocks:
            here = d_ref.at[(e & (HBL - 1)) >> 1, pl.ds(pl.multiple_of((e >> 4) * BLK, BLK), BLK), :]
            placed.append((here, jnp.where(upper == ((e & 1) == 1), block.astype(jnp.bfloat16), here[...])))
        for here, block in placed:
            here[...] = block

    def some(k, carry):
        start = pl.multiple_of(k * at_once, at_once)
        for t in range(BLK // 2):
            two = w_ref[pl.ds(start, at_once), 2 * BLK * t : 2 * BLK * (t + 1)].astype(jnp.float32)
            swapped = pltpu.roll(two, BLK, 1)
            if turned:
                even = jnp.where(low, two[:count], swapped[count:])
                odd = jnp.where(low, swapped[:count], two[count:])
            else:
                even, odd = jnp.where(low, two, swapped), jnp.where(low, swapped, two)
            lines[pl.ds(2 * t, count, stride=BLK), :] = even
            lines[pl.ds(2 * t + 1, count, stride=BLK), :] = odd
        for group in range(4):
            blocks = []
            for u in range(group // 2 * count // 2 + group % 2, (group // 2 + 1) * count // 2, 2):
                block = lines[u * BLK : (u + 1) * BLK, :]
                if turned:
                    both = jnp.concatenate([block, block], axis=0).T
                    blocks.append((dest[start + u], both[:BLK]))
                    blocks.append((dest[start + u + count], both[BLK:]))
                else:
                    blocks.append((dest[start + u], block))
            place(blocks)
        return carry

    lax.fori_loop(0, dest.shape[0] // at_once, some, 0)


def dense_weights(dest, weights, turned):
    whole = pl.BlockSpec(memory_space=pltpu.VMEM)
    return pl.pallas_call(
        functools.partial(dense_kernel, turned),
        out_shape=jax.ShapeDtypeStruct((8, D + BLK, 2 * BLK), jnp.bfloat16),
        in_specs=[pl.BlockSpec(memory_space=pltpu.SMEM), whole],
        out_specs=whole,
        scratch_shapes=[pltpu.VMEM((16 * BLK, 2 * BLK), jnp.float32)],
        compiler_params=pltpu.CompilerParams(vmem_limit_bytes=14 * MIB),
        cost_estimate=pl.CostEstimate(flops=0, transcendentals=0, bytes_accessed=20 << 20),
        name="dense_out" if turned else "dense_in",
    )(dest, weights)


def hidden_kernel(xc_ref, din_ref, dout_ref, both_ref):
    tok = xc_ref.shape[1] // 2
    x = jnp.concatenate([xc_ref[j, :tok, :] for j in range(16)], axis=1)
    c = jnp.concatenate([xc_ref[j, tok:, :] for j in range(16)], axis=1)

    def some(q, carry):
        win = jnp.concatenate([din_ref[2 * q + p, :D] for p in range(2)], axis=1)
        wout = jnp.concatenate([dout_ref[2 * q + p, :D] for p in range(2)], axis=1)
        v = jnp.dot(x, win, preferred_element_type=jnp.float32)
        g = jnp.dot(c, wout, preferred_element_type=jnp.float32)
        k0 = 0.7978845608028654
        t = jnp.tanh(k0 * (v + 0.044715 * (v * v * v)))
        rows = pl.ds(pl.multiple_of(q * 4 * BLK, 4 * BLK), 4 * BLK)
        both_ref[rows, tok:] = (0.5 * v * (1.0 + t)).T.astype(jnp.bfloat16)
        slope = 0.5 * (1.0 + t) + 0.5 * v * (1.0 - t * t) * (k0 * (1.0 + 3 * 0.044715 * (v * v)))
        both_ref[rows, :tok] = (g * slope).T.astype(jnp.bfloat16)
        return carry

    lax.fori_loop(0, 4, some, 0)


def hidden_stage(xc, din, dout, tok):
    cost = pl.CostEstimate(flops=4 * tok * D * 1024, transcendentals=tok * 1024, bytes_accessed=18 << 20)
    whole = pl.BlockSpec(memory_space=pltpu.VMEM)
    return pl.pallas_call(
        hidden_kernel,
        out_shape=jax.ShapeDtypeStruct((1024, 2 * tok), jnp.bfloat16),
        in_specs=[whole] * 3,
        out_specs=whole,
        compiler_params=pltpu.CompilerParams(vmem_limit_bytes=16 * MIB),
        cost_estimate=cost,
        name="hidden_stage",
    )(xc, din, dout)


def grad_kernel(scale, dest, send, first, last, xc_ref, both_ref, own_ref, other_ref, g_scr):
    tok = both_ref.shape[1] // 2
    unused = g_scr.shape[0] - 1
    most = 4
    g_scr[...] = jnp.zeros_like(g_scr)
    upper = lax.broadcasted_iota(jnp.int32, (tok, 2 * BLK), 1) >= BLK

    def some(j, carry):
        for q in range(4):
            begin, end = first[j * 4 + q], last[j * 4 + q]
            tile = xc_ref[j, :, q // 2 * 2 * BLK : (q // 2 + 1) * 2 * BLK].astype(jnp.float32)
            x, c = tile[:tok], tile[tok:]
            if q % 2:
                c = pltpu.roll(c, BLK, 1)
            else:
                x = pltpu.roll(x, BLK, 1)
            sides = jnp.concatenate([jnp.where(upper, x, 0.0), jnp.where(upper, 0.0, c)], axis=0).astype(jnp.bfloat16)
            blocks, targets = [], []
            for u in range(most):
                s = jnp.minimum(begin + u, unused - 1)
                at = pl.multiple_of((dest[s] & (HBL - 1)) * BLK, BLK)
                blocks.append(both_ref[pl.ds(at, BLK), :])
                targets.append(jnp.where(begin + u < end, send[s], unused))
            terms = jnp.dot(jnp.concatenate(blocks, axis=0), sides, preferred_element_type=jnp.float32)
            terms = (terms * scale).astype(jnp.bfloat16)
            for u in range(most):
                g_scr[targets[u]] = terms[u * BLK : (u + 1) * BLK]
        return carry

    lax.fori_loop(0, xc_ref.shape[0], some, 0)
    half = own_ref.shape[0]
    own_ref[...] = g_scr[:half]
    other_ref[...] = g_scr[half : 2 * half]


def grad_stage(tables, xc, both, slot_count, scale):
    tok = both.shape[1] // 2
    cost = pl.CostEstimate(flops=tok * D * 1024, transcendentals=0, bytes_accessed=7 << 20)
    smem = pl.BlockSpec(memory_space=pltpu.SMEM)
    whole = pl.BlockSpec(memory_space=pltpu.VMEM)
    half = (slot_count // 2, BLK, 2 * BLK)
    return pl.pallas_call(
        functools.partial(grad_kernel, scale),
        out_shape=(jax.ShapeDtypeStruct(half, jnp.bfloat16),) * 2,
        in_specs=[smem] * 4 + [whole] * 2,
        out_specs=(whole, whole),
        scratch_shapes=[pltpu.VMEM((slot_count + 1, BLK, 2 * BLK), jnp.bfloat16)],
        compiler_params=pltpu.CompilerParams(vmem_limit_bytes=10 * MIB),
        cost_estimate=cost,
        name="grad_stage",
    )(*tables, xc, both)


def part_kernel(quarter, din_ref, dout_ref, both_ref, *part_refs):
    tok = both_ref.shape[1] // 2
    size = 512
    for n, ref in enumerate(part_refs):

        def some(j, carry):
            rows = pl.ds(pl.multiple_of((quarter + n) * 1024 + j * size, size), size)
            win = jnp.concatenate([din_ref[p, rows, :] for p in range(8)], axis=1)
            wout = jnp.concatenate([dout_ref[p, rows, :] for p in range(8)], axis=1)
            out = jnp.dot(wout, both_ref[:, tok:], preferred_element_type=jnp.float32)
            back = jnp.dot(win, both_ref[:, :tok], preferred_element_type=jnp.float32)
            to = pl.ds(pl.multiple_of(j * size, size), size)
            ref[to, :] = jnp.concatenate([out, back], axis=1).astype(jnp.bfloat16)
            return carry

        lax.fori_loop(0, 1024 // size, some, 0)


def part_stage(din, dout, both, quarter, count):
    cost = pl.CostEstimate(
        flops=count * D * 1024 * both.shape[1] // 2, transcendentals=0, bytes_accessed=count * (9 << 19)
    )
    whole = pl.BlockSpec(memory_space=pltpu.VMEM)
    return pl.pallas_call(
        functools.partial(part_kernel, quarter),
        out_shape=(jax.ShapeDtypeStruct((1024, both.shape[1]), jnp.bfloat16),) * count,
        in_specs=[whole] * 3,
        out_specs=(whole,) * count,
        compiler_params=pltpu.CompilerParams(vmem_limit_bytes=12 * MIB),
        cost_estimate=cost,
    )(din, dout, both)


def turn_kernel(own_ref, out_ref, back_ref):
    own = own_ref[...].astype(jnp.float32)
    tok = out_ref.shape[0]
    out_ref[...] = own[:, :tok].T
    back_ref[...] = own[:, tok:].T


def own_turned(own):
    rows, cols = own.shape
    return pl.pallas_call(
        turn_kernel,
        out_shape=(jax.ShapeDtypeStruct((cols // 2, rows), jnp.float32),) * 2,
        compiler_params=pltpu.CompilerParams(vmem_limit_bytes=4 * MIB),
        name="own_turned",
    )(own)


def total_kernel(out_own_ref, back_own_ref, before_ref, after_ref, opposite_ref, out_ref, back_ref):
    refs = (before_ref, after_ref, opposite_ref)
    total = sum(ref[...].astype(jnp.float32) for ref in refs)
    tok = out_ref.shape[0]
    out_ref[...] = (out_own_ref[...] + total[:, :tok].T).astype(jnp.bfloat16)
    back_ref[...] = (back_own_ref[...] + total[:, tok:].T).astype(jnp.bfloat16)


def total_turned(own, terms):
    return pl.pallas_call(
        total_kernel,
        out_shape=tuple(jax.ShapeDtypeStruct(part.shape, jnp.bfloat16) for part in own),
        compiler_params=pltpu.CompilerParams(vmem_limit_bytes=6 * MIB),
        name="total_turned",
    )(*own, *terms)


def ring(axis, stride):
    def target(i, by):
        return i - i // stride % 4 * stride + (i // stride + by) % 4 * stride

    return tuple(
        functools.partial(lax.ppermute, axis_name=axis, perm=[(i, target(i, by)) for i in range(16)])
        for by in (1, 3, 2)
    )


def sent(block, ways):
    return [way(block) for way in ways]


def collect(blocks, up, down, over):
    own, before, after, opposite = blocks
    return own, up(after), down(before), over(opposite)


def added(*terms):
    return sum(term.astype(jnp.float32) for term in terms).astype(jnp.bfloat16)


def on_device(tokens, cotangent, block_cols, in_weights, out_weights):
    mp_at, dp_at = lax.axis_index("mp"), lax.axis_index("dp")
    slot_count = in_weights.shape[0]
    tok = tokens.shape[0]
    scale = float(tok * lax.axis_size("dp")) ** (-0.5)
    along_x, along_z, along_y = ring("mp", 4), ring("mp", 1), ring("dp", 2)
    block = jnp.concatenate([tokens, cotangent], axis=0)
    near = jnp.stack(sent(block, along_z))
    wide_own = sent(block, along_x)
    tables = slot_tables(block_cols, mp_at, dp_at, slot_count)
    wide = sent(near, along_x)
    pieces = [(own[None], others) for own, others in zip([block] + wide_own, [near] + wide)]
    xc = jnp.concatenate([piece for both in pieces for piece in both])
    dest, _ = lax.optimization_barrier((tables[0], near))
    din = dense_weights(dest, in_weights, False)
    dout = dense_weights(dest, out_weights, True)
    both = hidden_stage(xc, din, dout, tok)
    (opposite,) = part_stage(din, dout, both, 3, 1)
    opposite, both = lax.optimization_barrier((opposite, both))
    from_opposite = along_x[2](opposite)
    mine, other = grad_stage(tables, xc, both, slot_count, scale)
    other, both = lax.optimization_barrier((other, both))
    from_core = lax.ppermute(other, "dp", [(i, i ^ 1) for i in range(16)])
    own, before, after = part_stage(din, dout, both, 0, 3)
    from_core, _ = lax.optimization_barrier((from_core, before))
    across_terms = own, along_x[0](after), along_x[1](before), from_opposite
    share = slot_count // 32
    deep_way = functools.partial(lax.ppermute, axis_name="dp", perm=[(i, i ^ 8) for i in range(16)])

    def pair(at, count):
        return added(mine[at * share : (at + count) * share], from_core[at * share : (at + count) * share])

    late_own, late_other = pair(8, 4), pair(12, 4)
    late_deep = deep_way(late_other)
    deep_terms = collect([pair(2 * n, 2) for n in range(4)], *along_y)
    rows = own.shape[0] // 4
    across = [added(*(term[n * rows : (n + 1) * rows] for term in across_terms)) for n in range(4)]
    deep_terms, late_deep, _ = lax.optimization_barrier((deep_terms, late_deep, across[0]))
    to_deep = added(*(term[share:] for term in deep_terms))
    from_deep = deep_way(to_deep)
    late_terms = collect(
        [
            added(late_own[n * share : (n + 1) * share], late_deep[n * share : (n + 1) * share])
            for n in range(4)
        ],
        *along_y,
    )
    own_part = own_turned(across[0])
    near_terms = collect(across, *along_z)[1:]
    early = sum(term[:share].astype(jnp.float32) for term in deep_terms) + from_deep.astype(jnp.float32)
    late = sum(term.astype(jnp.float32) for term in late_terms)
    summed = jnp.concatenate([early, late])
    out_grad = summed[:, :, :BLK].reshape(-1, BLK * BLK)
    in_grad = summed[:, :, BLK:].swapaxes(1, 2).reshape(-1, BLK * BLK)
    near_terms, out_grad, in_grad = lax.optimization_barrier((near_terms, out_grad, in_grad))
    layer_out, token_grad = total_turned(own_part, near_terms)
    return (layer_out, token_grad, in_grad, out_grad)


def solution(mesh):
    placed = (P("dp", "mp"), P("dp", "mp"), P(), P("mp", None), P("mp", None))
    return jax.shard_map(
        on_device,
        mesh=mesh,
        in_specs=placed,
        out_specs=(P("dp", "mp"), P("dp", "mp"), P(("mp", "dp"), None), P(("mp", "dp"), None)),
        check_vma=False,
    )
```

```python
import functools

import jax
import jax.numpy as jnp
from jax import lax
from jax.experimental import pallas as pl
from jax.experimental.pallas import tpu as pltpu
from jax.sharding import PartitionSpec as P


D = 4096
BLK = 64
HBL = 16
MIB = 1024 * 1024


def place_of(steps):
    d = steps % 4
    return jnp.where(d == 0, 0, jnp.where(d == 3, 1, jnp.where(d == 1, 2, 3)))


def steps_of(place):
    return jnp.where(place == 0, 0, jnp.where(place == 1, 3, jnp.where(place == 2, 1, 2)))


def slot_tables(block_cols, mp_at, dp_at, slot_count):
    row_count, per_row = block_cols.shape
    flat_cols = block_cols.reshape(1, -1)
    is_mine = flat_cols // HBL == mp_at
    ranks = jnp.cumsum(is_mine.astype(jnp.int32), axis=1, dtype=jnp.int32) - 1
    targets = jnp.where(is_mine, ranks, slot_count)
    row_ids = lax.broadcasted_iota(jnp.int32, flat_cols.shape, 1) // per_row
    packed = row_ids * HBL + flat_cols - mp_at * HBL + 1
    slots = lax.broadcasted_iota(jnp.int32, (slot_count, 1), 0)
    found = jnp.sum(jnp.where(targets == slots, packed, 0), axis=1, dtype=jnp.int32)
    entry = jnp.where(found > 0, found - 1, row_count * HBL)
    place = lax.broadcasted_iota(jnp.int32, (row_count, 1), 0)
    owner = (mp_at // 4 + steps_of(place // 16)) % 4 * 4 + (mp_at % 4 + steps_of(place // 4 % 4)) % 4
    begin = (owner * 4 + place % 4) * HBL
    first = jnp.sum((entry[None, :] < begin).astype(jnp.int32), axis=1, dtype=jnp.int32)
    last = jnp.sum((entry[None, :] < begin + HBL).astype(jnp.int32), axis=1, dtype=jnp.int32)
    row = entry // HBL
    at = place_of(row // 16 - mp_at // 4) * 4 + place_of(row // 4 - mp_at % 4)
    dest = jnp.where(entry < row_count * HBL, (at * 4 + row % 4) * HBL + entry % HBL, row_count * HBL)
    slot = slots[:, 0]
    to = slot // 16
    core, across, deep = (to + dp_at) % 2, place_of(to // 2 - dp_at // 2 % 4), (to // 8 + dp_at // 8) % 2
    late = slot // 8 % 2
    owner_at = jnp.where(late == 0, across * 2 + deep, deep * 4 + across)
    send = ((core * 2 + late) * 8 + owner_at) * 8 + slot % 8
    return dest, send, first, last


def dense_kernel(turned, dest, w_ref, *refs):
    d_ref, lines = refs[-2:]
    if len(refs) == 2:
        d_ref[...] = jnp.zeros_like(d_ref)
    at_once = 16
    count = at_once // 2 if turned else at_once
    low = lax.broadcasted_iota(jnp.int32, (count, 2 * BLK), 1) < BLK
    upper = lax.broadcasted_iota(jnp.int32, (BLK, 2 * BLK), 1) >= BLK

    def place(blocks):
        placed = []
        for e, block in blocks:
            here = d_ref.at[(e & (HBL - 1)) >> 1, pl.ds(pl.multiple_of((e >> 4) * BLK, BLK), BLK), :]
            placed.append((here, jnp.where(upper == ((e & 1) == 1), block.astype(jnp.bfloat16), here[...])))
        for here, block in placed:
            here[...] = block

    def some(k, carry):
        start = pl.multiple_of(k * at_once, at_once)
        for t in range(BLK // 2):
            two = w_ref[pl.ds(start, at_once), 2 * BLK * t : 2 * BLK * (t + 1)].astype(jnp.float32)
            swapped = pltpu.roll(two, BLK, 1)
            if turned:
                even = jnp.where(low, two[:count], swapped[count:])
                odd = jnp.where(low, swapped[:count], two[count:])
            else:
                even, odd = jnp.where(low, two, swapped), jnp.where(low, swapped, two)
            lines[pl.ds(2 * t, count, stride=BLK), :] = even
            lines[pl.ds(2 * t + 1, count, stride=BLK), :] = odd
        for group in range(4):
            blocks = []
            for u in range(group // 2 * count // 2 + group % 2, (group // 2 + 1) * count // 2, 2):
                block = lines[u * BLK : (u + 1) * BLK, :]
                if turned:
                    both = jnp.concatenate([block, block], axis=0).T
                    blocks.append((dest[start + u], both[:BLK]))
                    blocks.append((dest[start + u + count], both[BLK:]))
                else:
                    blocks.append((dest[start + u], block))
            place(blocks)
        return carry

    lax.fori_loop(0, dest.shape[0] // at_once, some, 0)


def dense_weights(dest, weights, turned, *empty):
    whole = pl.BlockSpec(memory_space=pltpu.VMEM)
    return pl.pallas_call(
        functools.partial(dense_kernel, turned),
        out_shape=jax.ShapeDtypeStruct((8, D + BLK, 2 * BLK), jnp.bfloat16),
        in_specs=[pl.BlockSpec(memory_space=pltpu.SMEM), whole] + [whole] * len(empty),
        out_specs=whole,
        input_output_aliases={2: 0} if empty else {},
        scratch_shapes=[pltpu.VMEM((16 * BLK, 2 * BLK), jnp.float32)],
        compiler_params=pltpu.CompilerParams(vmem_limit_bytes=14 * MIB),
        cost_estimate=pl.CostEstimate(flops=0, transcendentals=0, bytes_accessed=20 << 20),
        name="dense_out" if turned else "dense_in",
    )(dest, weights, *empty)


def hidden_kernel(xc_ref, din_ref, dout_ref, both_ref):
    tok = xc_ref.shape[1] // 2
    x = jnp.concatenate([xc_ref[j, :tok, :] for j in range(16)], axis=1)
    c = jnp.concatenate([xc_ref[j, tok:, :] for j in range(16)], axis=1)

    def some(q, carry):
        win = jnp.concatenate([din_ref[2 * q + p, :D] for p in range(2)], axis=1)
        wout = jnp.concatenate([dout_ref[2 * q + p, :D] for p in range(2)], axis=1)
        v = jnp.dot(x, win, preferred_element_type=jnp.float32)
        g = jnp.dot(c, wout, preferred_element_type=jnp.float32)
        k0 = 0.7978845608028654
        t = jnp.tanh(k0 * (v + 0.044715 * (v * v * v)))
        rows = pl.ds(pl.multiple_of(q * 4 * BLK, 4 * BLK), 4 * BLK)
        both_ref[rows, tok:] = (0.5 * v * (1.0 + t)).T.astype(jnp.bfloat16)
        slope = 0.5 * (1.0 + t) + 0.5 * v * (1.0 - t * t) * (k0 * (1.0 + 3 * 0.044715 * (v * v)))
        both_ref[rows, :tok] = (g * slope).T.astype(jnp.bfloat16)
        return carry

    lax.fori_loop(0, 4, some, 0)


def hidden_stage(xc, din, dout, tok):
    cost = pl.CostEstimate(flops=4 * tok * D * 1024, transcendentals=tok * 1024, bytes_accessed=18 << 20)
    whole = pl.BlockSpec(memory_space=pltpu.VMEM)
    return pl.pallas_call(
        hidden_kernel,
        out_shape=jax.ShapeDtypeStruct((1024, 2 * tok), jnp.bfloat16),
        in_specs=[whole] * 3,
        out_specs=whole,
        compiler_params=pltpu.CompilerParams(vmem_limit_bytes=16 * MIB),
        cost_estimate=cost,
        name="hidden_stage",
    )(xc, din, dout)


def grad_kernel(scale, dest, send, first, last, xc_ref, both_ref, own_ref, other_ref, g_scr):
    tok = both_ref.shape[1] // 2
    unused = g_scr.shape[0] - 1
    most = 4
    g_scr[...] = jnp.zeros_like(g_scr)
    upper = lax.broadcasted_iota(jnp.int32, (tok, 2 * BLK), 1) >= BLK

    def some(j, carry):
        for q in range(4):
            begin, end = first[j * 4 + q], last[j * 4 + q]
            tile = xc_ref[j, :, q // 2 * 2 * BLK : (q // 2 + 1) * 2 * BLK].astype(jnp.float32)
            x, c = tile[:tok], tile[tok:]
            if q % 2:
                c = pltpu.roll(c, BLK, 1)
            else:
                x = pltpu.roll(x, BLK, 1)
            sides = jnp.concatenate([jnp.where(upper, x, 0.0), jnp.where(upper, 0.0, c)], axis=0).astype(jnp.bfloat16)
            blocks, targets = [], []
            for u in range(most):
                s = jnp.minimum(begin + u, unused - 1)
                at = pl.multiple_of((dest[s] & (HBL - 1)) * BLK, BLK)
                blocks.append(both_ref[pl.ds(at, BLK), :])
                targets.append(jnp.where(begin + u < end, send[s], unused))
            terms = jnp.dot(jnp.concatenate(blocks, axis=0), sides, preferred_element_type=jnp.float32)
            terms = (terms * scale).astype(jnp.bfloat16)
            for u in range(most):
                g_scr[targets[u]] = terms[u * BLK : (u + 1) * BLK]
        return carry

    lax.fori_loop(0, xc_ref.shape[0], some, 0)
    half = own_ref.shape[0]
    own_ref[...] = g_scr[:half]
    other_ref[...] = g_scr[half : 2 * half]


def grad_stage(tables, xc, both, slot_count, scale):
    tok = both.shape[1] // 2
    cost = pl.CostEstimate(flops=tok * D * 1024, transcendentals=0, bytes_accessed=7 << 20)
    smem = pl.BlockSpec(memory_space=pltpu.SMEM)
    whole = pl.BlockSpec(memory_space=pltpu.VMEM)
    half = (slot_count // 2, BLK, 2 * BLK)
    return pl.pallas_call(
        functools.partial(grad_kernel, scale),
        out_shape=(jax.ShapeDtypeStruct(half, jnp.bfloat16),) * 2,
        in_specs=[smem] * 4 + [whole] * 2,
        out_specs=(whole, whole),
        scratch_shapes=[pltpu.VMEM((slot_count + 1, BLK, 2 * BLK), jnp.bfloat16)],
        compiler_params=pltpu.CompilerParams(vmem_limit_bytes=10 * MIB),
        cost_estimate=cost,
        name="grad_stage",
    )(*tables, xc, both)


def part_kernel(quarter, din_ref, dout_ref, both_ref, *part_refs):
    tok = both_ref.shape[1] // 2
    size = 512
    for n, ref in enumerate(part_refs):

        def some(j, carry):
            rows = pl.ds(pl.multiple_of((quarter + n) * 1024 + j * size, size), size)
            win = jnp.concatenate([din_ref[p, rows, :] for p in range(8)], axis=1)
            wout = jnp.concatenate([dout_ref[p, rows, :] for p in range(8)], axis=1)
            out = jnp.dot(wout, both_ref[:, tok:], preferred_element_type=jnp.float32)
            back = jnp.dot(win, both_ref[:, :tok], preferred_element_type=jnp.float32)
            to = pl.ds(pl.multiple_of(j * size, size), size)
            ref[to, :] = jnp.concatenate([out, back], axis=1).astype(jnp.bfloat16)
            return carry

        lax.fori_loop(0, 1024 // size, some, 0)


def part_stage(din, dout, both, quarter, count):
    cost = pl.CostEstimate(
        flops=count * D * 1024 * both.shape[1] // 2, transcendentals=0, bytes_accessed=count * (9 << 19)
    )
    whole = pl.BlockSpec(memory_space=pltpu.VMEM)
    return pl.pallas_call(
        functools.partial(part_kernel, quarter),
        out_shape=(jax.ShapeDtypeStruct((1024, both.shape[1]), jnp.bfloat16),) * count,
        in_specs=[whole] * 3,
        out_specs=(whole,) * count,
        compiler_params=pltpu.CompilerParams(vmem_limit_bytes=12 * MIB),
        cost_estimate=cost,
    )(din, dout, both)


def turn_kernel(own_ref, out_ref, back_ref):
    own = own_ref[...].astype(jnp.float32)
    tok = out_ref.shape[0]
    out_ref[...] = own[:, :tok].T
    back_ref[...] = own[:, tok:].T


def own_turned(own):
    rows, cols = own.shape
    return pl.pallas_call(
        turn_kernel,
        out_shape=(jax.ShapeDtypeStruct((cols // 2, rows), jnp.float32),) * 2,
        compiler_params=pltpu.CompilerParams(vmem_limit_bytes=4 * MIB),
        name="own_turned",
    )(own)


def total_kernel(out_own_ref, back_own_ref, before_ref, after_ref, opposite_ref, out_ref, back_ref):
    refs = (before_ref, after_ref, opposite_ref)
    total = sum(ref[...].astype(jnp.float32) for ref in refs)
    tok = out_ref.shape[0]
    out_ref[...] = (out_own_ref[...] + total[:, :tok].T).astype(jnp.bfloat16)
    back_ref[...] = (back_own_ref[...] + total[:, tok:].T).astype(jnp.bfloat16)


def total_turned(own, terms):
    return pl.pallas_call(
        total_kernel,
        out_shape=tuple(jax.ShapeDtypeStruct(part.shape, jnp.bfloat16) for part in own),
        compiler_params=pltpu.CompilerParams(vmem_limit_bytes=6 * MIB),
        name="total_turned",
    )(*own, *terms)


def ring(axis, stride):
    def target(i, by):
        return i - i // stride % 4 * stride + (i // stride + by) % 4 * stride

    return tuple(
        functools.partial(lax.ppermute, axis_name=axis, perm=[(i, target(i, by)) for i in range(16)])
        for by in (1, 3, 2)
    )


def sent(block, ways):
    return [way(block) for way in ways]


def collect(blocks, up, down, over):
    own, before, after, opposite = blocks
    return own, up(after), down(before), over(opposite)


def added(*terms):
    return sum(term.astype(jnp.float32) for term in terms).astype(jnp.bfloat16)


def on_device(tokens, cotangent, block_cols, in_weights, out_weights):
    mp_at, dp_at = lax.axis_index("mp"), lax.axis_index("dp")
    slot_count = in_weights.shape[0]
    tok = tokens.shape[0]
    scale = float(tok * lax.axis_size("dp")) ** (-0.5)
    along_x, along_z, along_y = ring("mp", 4), ring("mp", 1), ring("dp", 2)
    block = jnp.concatenate([tokens, cotangent], axis=0)
    near = jnp.stack(sent(block, along_z))
    wide_own = sent(block, along_x)
    tables = slot_tables(block_cols, mp_at, dp_at, slot_count)
    wide = sent(near, along_x)
    pieces = [(own[None], others) for own, others in zip([block] + wide_own, [near] + wide)]
    xc = jnp.concatenate([piece for both in pieces for piece in both])
    dest, _ = lax.optimization_barrier((tables[0], near))
    empty = jnp.zeros((8, D + BLK, 2 * BLK), jnp.bfloat16)
    din = dense_weights(dest, in_weights, False)
    dout = dense_weights(dest, out_weights, True, empty)
    both = hidden_stage(xc, din, dout, tok)
    (opposite,) = part_stage(din, dout, both, 3, 1)
    opposite, both = lax.optimization_barrier((opposite, both))
    from_opposite = along_x[2](opposite)
    mine, other = grad_stage(tables, xc, both, slot_count, scale)
    other, both = lax.optimization_barrier((other, both))
    from_core = lax.ppermute(other, "dp", [(i, i ^ 1) for i in range(16)])
    own, before, after = part_stage(din, dout, both, 0, 3)
    from_core, _ = lax.optimization_barrier((from_core, before))
    across_terms = own, along_x[0](after), along_x[1](before), from_opposite
    share = slot_count // 32
    deep_way = functools.partial(lax.ppermute, axis_name="dp", perm=[(i, i ^ 8) for i in range(16)])

    def pair(at, count):
        return added(mine[at * share : (at + count) * share], from_core[at * share : (at + count) * share])

    late_own, late_other = pair(8, 4), pair(12, 4)
    late_deep = deep_way(late_other)
    deep_terms = collect([pair(2 * n, 2) for n in range(4)], *along_y)
    rows = own.shape[0] // 4
    across = [added(*(term[n * rows : (n + 1) * rows] for term in across_terms)) for n in range(4)]
    deep_terms, late_deep, _ = lax.optimization_barrier((deep_terms, late_deep, across[0]))
    to_deep = added(*(term[share:] for term in deep_terms))
    from_deep = deep_way(to_deep)
    late_terms = collect(
        [
            added(late_own[n * share : (n + 1) * share], late_deep[n * share : (n + 1) * share])
            for n in range(4)
        ],
        *along_y,
    )
    own_part = own_turned(across[0])
    near_terms = collect(across, *along_z)[1:]
    early = sum(term[:share].astype(jnp.float32) for term in deep_terms) + from_deep.astype(jnp.float32)
    late = sum(term.astype(jnp.float32) for term in late_terms)
    summed = jnp.concatenate([early, late])
    out_grad = summed[:, :, :BLK].reshape(-1, BLK * BLK)
    in_grad = summed[:, :, BLK:].swapaxes(1, 2).reshape(-1, BLK * BLK)
    near_terms, out_grad, in_grad = lax.optimization_barrier((near_terms, out_grad, in_grad))
    layer_out, token_grad = total_turned(own_part, near_terms)
    return (layer_out, token_grad, in_grad, out_grad)


def solution(mesh):
    placed = (P("dp", "mp"), P("dp", "mp"), P(), P("mp", None), P("mp", None))
    return jax.shard_map(
        on_device,
        mesh=mesh,
        in_specs=placed,
        out_specs=(P("dp", "mp"), P("dp", "mp"), P(("mp", "dp"), None), P(("mp", "dp"), None)),
        check_vma=False,
    )
```
